32 devices in a mesh: dp: 8 (over y, x, core), tensor: 4 (over z).
Axes of the slice: x: 2, y: 2, z: 4, core: 2. Of those that a mesh axis runs over, the one named last changes fastest.
Arguments:
- hidden: bfloat16 [4096, 8192], P('dp'), may hold values from -24 to 24
- weight: bfloat16 [1024, 8192], P('tensor', 'dp'), may hold values from -2 to 2, as said below
- qk_scale: float32 [4, 128], P('tensor'), may hold values from 0.5 to 2
- cotangent: bfloat16 [4096, 1024], P('dp', 'tensor'), may hold values from -12 to 12
Outputs:
- keys_values: bfloat16 [4096, 1024], P('dp', 'tensor')
- input_grad: bfloat16 [4096, 8192], P(('dp', 'tensor'))
- new_weight: bfloat16 [1024, 8192], P('tensor', 'dp')
The draws below stay inside these ranges and needn't reach their ends.
Inputs may be any that keep to these rules, and one draw needn't show every extreme that they name: Entries of weight are of order 8192 ** -0.5 times a row scale.
All inputs are finite; a program needn't handle non-finite values.
Results may differ from the reference program's by a relative error of at most 0.009.
Values may be sent and summed in bfloat16 or wider, within the bound.
No kernel may reach another device: no remote copies, remote signals or barrier semaphores. Data moves between devices by JAX's collectives and lax.ppermute only.
A program may use at most 128 MiB of HBM per device.

```python
import math
import jax
import jax.numpy as jnp
from jax import lax

D = 8192
HD = 128
KVH = 4
TOK = 512
TOKENS = 4096
N_TENSOR = 4


def make_hidden(key):
    first, second = jax.random.split(key)
    blocks = TOKENS // TOK
    width_block = D // blocks
    noise = jnp.clip(jax.random.normal(first, (TOKENS, D), jnp.float32), -6.0, 6.0)
    pairing = jax.random.permutation(second, blocks)
    token_block = jnp.arange(TOKENS, dtype=jnp.int32) // TOK
    column_block = jnp.arange(D, dtype=jnp.int32) // width_block
    partner = jnp.take(pairing, token_block)
    boosted = jnp.where(partner[:, None] == column_block[None, :], 4.0 * noise, noise)
    return boosted.astype(jnp.bfloat16)


def make_weight(key):
    first, second = jax.random.split(key, 2)
    rows = KVH * 2 * HD
    row_scale = jnp.exp(jax.random.uniform(second, (rows, 1), jnp.float32, math.log(0.3), math.log(3.0)))
    ramp = 10.0 ** (0.5 * (jnp.arange(D, dtype=jnp.float32) / D - 1.0))
    noise = jnp.clip(jax.random.normal(first, (rows, D), jnp.float32), -6.0, 6.0)
    return (noise * row_scale * ramp[None, :] * D ** (-0.5)).astype(jnp.bfloat16)


def draw_hidden(key, part):
    return make_hidden(jax.random.fold_in(key, 11))


def draw_weight(key, part):
    return make_weight(jax.random.fold_in(key, 12))


def draw_cotangent(key, part):
    states = make_hidden(jax.random.fold_in(key, 11)).astype(jnp.float32)
    rows_all = make_weight(jax.random.fold_in(key, 12)).astype(jnp.float32)
    value_rows = rows_all.reshape(KVH, 2, HD, D)[:, 1].reshape(KVH * HD, D)
    row_length = jnp.sqrt(jnp.sum(value_rows * value_rows, 1))
    raw_values = jnp.dot(states, value_rows.T, precision=lax.Precision.HIGHEST)
    aligned = jnp.clip(raw_values / row_length[None, :], -8.0, 8.0).reshape(TOKENS, KVH, 1, HD)
    noise = jnp.clip(jax.random.normal(jax.random.fold_in(key, 13), (TOKENS, KVH, 2, HD), jnp.float32), -6.0, 6.0)
    coupling = 0.5 * math.sqrt(D / TOKENS)
    extra = jnp.concatenate([jnp.zeros_like(aligned), coupling * aligned], 2)
    return (noise + extra).reshape(TOKENS, KVH * 2 * HD).astype(jnp.bfloat16)


def block_levels(stream_key, extent, pieces, smallest, high):
    loudness, own = 1.0, jax.random.fold_in(stream_key, 6)
    for axis_at, shards_of in pieces:
        steps = jnp.exp(jax.random.uniform(jax.random.fold_in(own, axis_at), (shards_of,), jnp.float32, smallest / len(pieces), high / len(pieces)))
        loudness = loudness * jnp.repeat(steps, extent[axis_at] // shards_of).reshape([-1 if axis == axis_at else 1 for axis in range(len(extent))])
    return loudness


def setup_inputs(seed: int = 0) -> dict:
    key_list = jax.random.split(jax.random.key(seed), 5)
    hidden = draw_hidden(jax.random.fold_in(key_list[4], 71), 0)
    weight = draw_weight(jax.random.fold_in(key_list[4], 71), 0)
    qk_scale = jnp.clip(jnp.exp(math.log(2.0) - 1.3862944 * jax.random.uniform(key_list[2], (KVH, HD), jnp.float32) ** block_levels(key_list[2], (KVH, HD), ((0, 4),), -0.2, 0.2)), 0.5, 2.0)
    cotangent = draw_cotangent(jax.random.fold_in(key_list[4], 71), 0)
    return dict(hidden=hidden, weight=weight, qk_scale=qk_scale, cotangent=cotangent)


step_rate = 0.5
epsilon = 1e-06

def keys_and_grads(raw, qk_scale, cotangent):
    tok = raw.shape[0]
    heads = qk_scale.shape[0]
    size = qk_scale.shape[1]
    parts = raw.reshape(tok, heads, 2, size)
    key_raw = parts[:, :, 0]
    values = parts[:, :, 1]
    length = jnp.sqrt(lax.optimization_barrier(jnp.sum(key_raw * key_raw, -1, keepdims=True)) + epsilon)
    unit = key_raw / length
    factor = qk_scale * math.sqrt(size)
    keys = factor * unit
    outputs = jnp.stack([keys, values], 2).reshape(tok, -1).astype(jnp.bfloat16)
    cot = cotangent.astype(jnp.float32).reshape(tok, heads, 2, size)
    along = factor * cot[:, :, 0]
    key_grad = (along - unit * lax.optimization_barrier(jnp.sum(unit * along, -1, keepdims=True))) / length
    d_raw = jnp.stack([key_grad, cot[:, :, 1]], 2).reshape(tok, -1).astype(jnp.bfloat16)
    return (outputs, d_raw)

def reference(hidden, weight, qk_scale, cotangent):
    raw = jnp.dot(hidden, weight.T, preferred_element_type=jnp.float32)
    keys_values, d_raw = keys_and_grads(raw, qk_scale, cotangent)
    grad = jnp.dot(d_raw.T, hidden, preferred_element_type=jnp.float32)
    block = weight.shape[0] // N_TENSOR
    total = jnp.zeros(hidden.shape, jnp.float32)
    for index in range(N_TENSOR):
        part_sum = jnp.dot(d_raw[:, index * block:(index + 1) * block], weight[index * block:(index + 1) * block], preferred_element_type=jnp.float32)
        rounded = lax.optimization_barrier(part_sum.astype(jnp.bfloat16))
        total = total + rounded.astype(jnp.float32)
    input_grad = total.astype(jnp.bfloat16)
    w_rows = weight.astype(jnp.float32)
    grad_dot = lax.optimization_barrier(jnp.sum(grad * w_rows, 1, keepdims=True))
    w_square = lax.optimization_barrier(jnp.sum(w_rows * w_rows, 1, keepdims=True))
    g_square = lax.optimization_barrier(jnp.sum(grad * grad, 1, keepdims=True))
    tangent = grad - grad_dot / w_square * w_rows
    moved = w_rows - step_rate * jnp.sqrt(w_square / (g_square + epsilon)) * tangent
    norm_sq = lax.optimization_barrier(jnp.sum(moved * moved, 1, keepdims=True))
    new_weight = (math.sqrt(weight.shape[1]) * moved / jnp.sqrt(norm_sq)).astype(jnp.bfloat16)
    return (keys_values, input_grad, new_weight)
```

```python
import math

import jax
import jax.numpy as jnp
from jax import lax
from jax.experimental import pallas as pl
from jax.experimental.pallas import tpu as pltpu
from jax.sharding import PartitionSpec as P

step_rate = 0.5
epsilon = 1e-06
F32 = jnp.float32
BF16 = jnp.bfloat16


def swap(x, bit, n_dp):
    return lax.ppermute(x, "dp", [(i, i ^ bit) for i in range(n_dp)])


def gather_blocks(w, n_dp):
    bits = [1 << i for i in range(1, n_dp.bit_length() - 1)]
    half = w.shape[0] // 2
    parts = []
    for rows, order in ((w[:half], bits), (w[half:], bits[::-1])):
        have = {0: rows}
        for bit in order:
            have.update({r ^ bit: swap(x, bit, n_dp) for r, x in list(have.items())})
        have.update({r ^ 1: swap(x, 1, n_dp) for r, x in list(have.items())})
        parts.append(have)
    return parts


def project(hidden, parts, qk_scale, cotangent, where):
    tok = hidden.shape[0]
    n_blocks = len(parts[0])
    half, width = parts[0][0].shape
    rows = 2 * half
    heads, size = qk_scale.shape

    def body(where_ref, h_ref, s_ref, c_ref, *rest):
        w_refs = rest[: 2 * n_blocks]
        out_ref, d_ref, dt_ref, acc = rest[2 * n_blocks :]
        step = pl.program_id(0)
        for r in range(n_blocks):

            @pl.when(step == r)
            def _():
                for side in range(2):
                    part = lax.dot_general(
                        h_ref[...], w_refs[2 * r + side][...], (((1,), (1,)), ((), ())), preferred_element_type=F32
                    )
                    at = slice(side * half, (side + 1) * half)
                    if r == 0:
                        acc[:, at] = part
                    else:
                        acc[:, at] += part

        @pl.when(step == n_blocks - 1)
        def _():
            for h in range(heads):
                k_at = slice(2 * h * size, (2 * h + 1) * size)
                v_at = slice((2 * h + 1) * size, (2 * h + 2) * size)
                key_raw = acc[:, k_at]
                length = jnp.sqrt(jnp.sum(key_raw * key_raw, -1, keepdims=True) + epsilon)
                unit = key_raw / length
                factor = s_ref[h : h + 1, :] * math.sqrt(size)
                out_ref[:, k_at] = (factor * unit).astype(BF16)
                out_ref[:, v_at] = acc[:, v_at].astype(BF16)
                along = factor * c_ref[:, k_at].astype(F32)
                grad = (along - unit * jnp.sum(unit * along, -1, keepdims=True)) / length
                d_ref[:, k_at] = grad.astype(BF16)
                d_ref[:, v_at] = c_ref[:, v_at]
                dt_ref[k_at, :] = grad.T.astype(BF16)
                dt_ref[v_at, :] = c_ref[:, v_at].astype(F32).T.astype(BF16)

    fixed = lambda i, where_ref: (0, 0)
    return pl.pallas_call(
        body,
        grid_spec=pltpu.PrefetchScalarGridSpec(
            num_scalar_prefetch=1,
            grid=(n_blocks,),
            in_specs=[
                pl.BlockSpec((tok, width), lambda i, where_ref: (0, where_ref[0] ^ i)),
                pl.BlockSpec((heads, size), fixed),
                pl.BlockSpec((tok, rows), fixed),
            ]
            + [pl.BlockSpec((half, width), fixed)] * (2 * n_blocks),
            out_specs=[
                pl.BlockSpec((tok, rows), fixed),
                pl.BlockSpec((tok, rows), fixed),
                pl.BlockSpec((rows, tok), fixed),
            ],
            scratch_shapes=[pltpu.VMEM((tok, rows), F32)],
        ),
        out_shape=[
            jax.ShapeDtypeStruct((tok, rows), BF16),
            jax.ShapeDtypeStruct((tok, rows), BF16),
            jax.ShapeDtypeStruct((rows, tok), BF16),
        ],
        name="project",
    )(where, hidden, qk_scale, cotangent, *[parts[s][r] for r in range(n_blocks) for s in range(2)])


def weight_grad(d_t, hidden, where, n_blocks, odd, dtype):
    rows, tok = d_t.shape
    width = hidden.shape[1] // n_blocks

    def body(where_ref, d_ref, h_ref, out_ref):
        out_ref[0] = jnp.dot(d_ref[...], h_ref[...], preferred_element_type=F32).astype(dtype)

    return pl.pallas_call(
        body,
        grid_spec=pltpu.PrefetchScalarGridSpec(
            num_scalar_prefetch=1,
            grid=(n_blocks // 2,),
            in_specs=[
                pl.BlockSpec((rows, tok), lambda i, where_ref: (0, 0)),
                pl.BlockSpec((tok, width), lambda i, where_ref: (0, where_ref[0] ^ (2 * i + odd))),
            ],
            out_specs=pl.BlockSpec((1, rows, width), lambda i, where_ref: (i, 0, 0)),
        ),
        out_shape=jax.ShapeDtypeStruct((n_blocks // 2, rows, width), dtype),
        name="weight_grad_odd" if odd else "weight_grad_even",
    )(where, d_t, hidden)


def hidden_grad(d_raw, parts, where):
    tok = d_raw.shape[0]
    n_blocks = len(parts[0])
    half, width = parts[0][0].shape

    def body(where_ref, d_ref, *rest):
        w_refs, out_ref = rest[:-1], rest[-1]
        step = pl.program_id(0)
        for r in range(n_blocks):

            @pl.when(step == r)
            def _():
                w = jnp.concatenate([w_refs[2 * r][...], w_refs[2 * r + 1][...]], 0)
                out_ref[...] = jnp.dot(d_ref[...], w, preferred_element_type=F32).astype(BF16)

    fixed = lambda i, where_ref: (0, 0)
    return pl.pallas_call(
        body,
        grid_spec=pltpu.PrefetchScalarGridSpec(
            num_scalar_prefetch=1,
            grid=(n_blocks,),
            in_specs=[pl.BlockSpec(d_raw.shape, fixed)] + [pl.BlockSpec((half, width), fixed)] * (2 * n_blocks),
            out_specs=pl.BlockSpec((tok, width), lambda i, where_ref: (0, where_ref[0] ^ i)),
        ),
        out_shape=jax.ShapeDtypeStruct((tok, n_blocks * width), BF16),
        name="hidden_grad",
    )(where, d_raw, *[parts[s][r] for r in range(n_blocks) for s in range(2)])


def scatter_sum(keep, sent, n_dp):
    total = keep + swap(sent, 1, n_dp).astype(F32)
    count = n_dp.bit_length() - 2
    rows, width = keep.shape[1:]
    total = total.reshape((2,) * count + (rows, width))
    half = rows // 2
    sides = []
    for at, order in ((0, list(range(count))), (half, list(range(count))[::-1])):
        part = lax.slice_in_dim(total, at, at + half, axis=count)
        left = list(range(count))[::-1]
        for b in order:
            axis = left.index(b)
            left.remove(b)
            go = lax.index_in_dim(part, 1, axis, keepdims=False).astype(BF16)
            stay = lax.index_in_dim(part, 0, axis, keepdims=False)
            part = stay + swap(go, 2 << b, n_dp).astype(F32)
        sides.append(part)
    return jnp.concatenate(sides, 0)


def local(hidden, weight, qk_scale, cotangent, n_dp):
    where = lax.axis_index("dp").astype(jnp.int32).reshape(1)
    parts = gather_blocks(weight, n_dp)
    keys_values, d_raw, d_t = project(hidden, parts, qk_scale, cotangent, where)
    sent = weight_grad(d_t, hidden, where, n_dp, 1, BF16)
    input_share = hidden_grad(d_raw, parts, where)
    keep = weight_grad(d_t, hidden, where, n_dp, 0, F32)
    input_grad = lax.psum_scatter(input_share, "tensor", scatter_dimension=0, tiled=True)
    grad = scatter_sum(keep, sent, n_dp)
    w = weight.astype(F32)
    sums = jnp.stack([jnp.sum(grad * w, 1), jnp.sum(w * w, 1), jnp.sum(grad * grad, 1)])
    bit = 1
    while bit < n_dp:
        sums = sums + swap(sums, bit, n_dp)
        bit *= 2
    gw, ww, gg = sums[0], sums[1], sums[2]
    ratio = gw / ww
    rate = step_rate * jnp.sqrt(ww / (gg + epsilon))
    norm_sq = ww + rate * rate * (gg - ratio * gw)
    scale = math.sqrt(n_dp * weight.shape[1]) / jnp.sqrt(norm_sq)
    moved = w - rate[:, None] * (grad - ratio[:, None] * w)
    new_weight = (scale[:, None] * moved).astype(BF16)
    return (keys_values, input_grad, new_weight)


def solution(mesh):
    in_specs = (P("dp", None), P("tensor", "dp"), P("tensor", None), P("dp", "tensor"))
    out_specs = (P("dp", "tensor"), P(("dp", "tensor"), None), P("tensor", "dp"))
    n_dp = mesh.shape["dp"]

    def body(hidden, weight, qk_scale, cotangent):
        return local(hidden, weight, qk_scale, cotangent, n_dp)

    return jax.shard_map(body, mesh=mesh, in_specs=in_specs, out_specs=out_specs, check_vma=False)
```

```python
import math

import jax
import jax.numpy as jnp
from jax import lax
from jax.experimental import pallas as pl
from jax.experimental.pallas import tpu as pltpu
from jax.sharding import PartitionSpec as P

step_rate = 0.5
epsilon = 1e-06
F32 = jnp.float32
BF16 = jnp.bfloat16


def swap(x, bit, n_dp):
    return lax.ppermute(x, "dp", [(i, i ^ bit) for i in range(n_dp)])


def gather_blocks(w, n_dp):
    bits = [1 << i for i in range(1, n_dp.bit_length() - 1)]
    half = w.shape[0] // 2
    parts = []
    for rows, order in ((w[:half], bits), (w[half:], bits[::-1])):
        have = {0: rows}
        for bit in order:
            have.update({r ^ bit: swap(x, bit, n_dp) for r, x in list(have.items())})
        have.update({r ^ 1: swap(x, 1, n_dp) for r, x in list(have.items())})
        parts.append(have)
    return parts


def project(hidden, parts, qk_scale, cotangent, where, n_tensor):
    tok = hidden.shape[0]
    n_blocks = len(parts[0])
    half, width = parts[0][0].shape
    rows = 2 * half
    heads, size = qk_scale.shape
    chunk = tok // n_tensor

    def body(where_ref, h_ref, s_ref, c_ref, *rest):
        w_refs = rest[: 2 * n_blocks]
        out_ref, d_ref, dt_ref, acc = rest[2 * n_blocks :]
        step = pl.program_id(0)
        for r in range(n_blocks):

            @pl.when(step == r)
            def _():
                w = jnp.concatenate([w_refs[2 * r][...], w_refs[2 * r + 1][...]], 0)
                part = lax.dot_general(h_ref[...], w, (((1,), (1,)), ((), ())), preferred_element_type=F32)
                if r == 0:
                    acc[...] = part
                else:
                    acc[...] += part

        @pl.when(step == n_blocks - 1)
        def _():
            for h in range(heads):
                k_at = slice(2 * h * size, (2 * h + 1) * size)
                v_at = slice((2 * h + 1) * size, (2 * h + 2) * size)
                key_raw = acc[:, k_at]
                length = jnp.sqrt(jnp.sum(key_raw * key_raw, -1, keepdims=True) + epsilon)
                unit = key_raw / length
                factor = s_ref[h : h + 1, :] * math.sqrt(size)
                out_ref[:, k_at] = (factor * unit).astype(BF16)
                out_ref[:, v_at] = acc[:, v_at].astype(BF16)
                along = factor * c_ref[:, k_at].astype(F32)
                grad = (along - unit * jnp.sum(unit * along, -1, keepdims=True)) / length
                for j in range(n_tensor):
                    slot = lax.rem(where_ref[1] + (n_tensor - j), n_tensor)
                    at = slice(j * chunk, (j + 1) * chunk)
                    d_ref[slot, :, k_at] = grad[at].astype(BF16)
                    d_ref[slot, :, v_at] = c_ref[at, v_at]
                dt_ref[k_at, :] = grad.T.astype(BF16)
                dt_ref[v_at, :] = c_ref[:, v_at].astype(F32).T.astype(BF16)

    fixed = lambda i, where_ref: (0, 0)
    return pl.pallas_call(
        body,
        grid_spec=pltpu.PrefetchScalarGridSpec(
            num_scalar_prefetch=1,
            grid=(n_blocks,),
            in_specs=[
                pl.BlockSpec((tok, width), lambda i, where_ref: (0, where_ref[0] ^ i)),
                pl.BlockSpec((heads, size), fixed),
                pl.BlockSpec((tok, rows), fixed),
            ]
            + [pl.BlockSpec((half, width), fixed)] * (2 * n_blocks),
            out_specs=[
                pl.BlockSpec((tok, rows), fixed),
                pl.BlockSpec((n_tensor, chunk, rows), lambda i, where_ref: (0, 0, 0)),
                pl.BlockSpec((rows, tok), fixed),
            ],
            scratch_shapes=[pltpu.VMEM((tok, rows), F32)],
        ),
        out_shape=[
            jax.ShapeDtypeStruct((tok, rows), BF16),
            jax.ShapeDtypeStruct((n_tensor, chunk, rows), BF16),
            jax.ShapeDtypeStruct((rows, tok), BF16),
        ],
        name="project",
    )(where, hidden, qk_scale, cotangent, *[parts[s][r] for r in range(n_blocks) for s in range(2)])


def weight_grad(d_t, hidden, where, n_blocks, odd, dtype):
    rows, tok = d_t.shape
    width = hidden.shape[1] // n_blocks

    def body(where_ref, d_ref, h_ref, out_ref):
        out_ref[0] = jnp.dot(d_ref[...], h_ref[...], preferred_element_type=F32).astype(dtype)

    return pl.pallas_call(
        body,
        grid_spec=pltpu.PrefetchScalarGridSpec(
            num_scalar_prefetch=1,
            grid=(n_blocks // 2,),
            in_specs=[
                pl.BlockSpec((rows, tok), lambda i, where_ref: (0, 0)),
                pl.BlockSpec((tok, width), lambda i, where_ref: (0, where_ref[0] ^ (2 * i + odd))),
            ],
            out_specs=pl.BlockSpec((1, rows, width), lambda i, where_ref: (i, 0, 0)),
        ),
        out_shape=jax.ShapeDtypeStruct((n_blocks // 2, rows, width), dtype),
        name="weight_grad_odd" if odd else "weight_grad_even",
    )(where, d_t, hidden)


def shift(x, by, n_tensor):
    return lax.ppermute(x, "tensor", [(i, (i - by) % n_tensor) for i in range(n_tensor)])


def gather_others(w, n_tensor, n_dp):
    half = w.shape[0] // 2
    slots = {1: shift(w, 1, n_tensor), n_tensor - 1: shift(w, -1, n_tensor)}
    for k in range(2, n_tensor - 1):
        low = shift(slots[1][:half], k - 1, n_tensor)
        high = shift(slots[n_tensor - 1][half:], k + 1, n_tensor)
        slots[k] = jnp.concatenate([low, high], 0)
    rest = {}
    bit = 2
    while bit < n_dp:
        for k, x in slots.items():
            rest[bit, k] = swap(x, bit, n_dp)
        bit *= 2
    rest.update({(0, k): x for k, x in slots.items()})
    rest.update({(r ^ 1, k): swap(x, 1, n_dp) for (r, k), x in list(rest.items())})
    return rest


def hidden_share(d_slots, parts, blocks):
    n_tensor, chunk, rows = d_slots.shape
    half, width = parts[0][0].shape

    def body(d_ref, *rest):
        w_refs, out_ref = rest[:-1], rest[-1]
        step = pl.program_id(0)
        d = d_ref[...].reshape(n_tensor * chunk, rows)
        for i in range(len(blocks)):

            @pl.when(step == i)
            def _():
                w = jnp.concatenate([w_refs[2 * i][...], w_refs[2 * i + 1][...]], 0)
                out = jnp.dot(d, w, preferred_element_type=F32).astype(BF16)
                out_ref[...] = out.reshape(n_tensor, chunk, width)

    return pl.pallas_call(
        body,
        grid=(len(blocks),),
        in_specs=[pl.BlockSpec(d_slots.shape, lambda i: (0, 0, 0))]
        + [pl.BlockSpec((half, width), lambda i: (0, 0))] * (2 * len(blocks)),
        out_specs=pl.BlockSpec((n_tensor, chunk, width), lambda i: (0, 0, i)),
        out_shape=jax.ShapeDtypeStruct((n_tensor, chunk, len(blocks) * width), BF16),
        name="hidden_share",
    )(d_slots, *[parts[s][r] for r in blocks for s in range(2)])


def hidden_grad(d_own, d_rest, parts, others, where, blocks, into):
    n_tensor = len(d_rest) + 1
    chunk, rows = d_own.shape
    half, width = parts[0][0].shape
    n_blocks = len(parts[0])
    per = n_tensor + 1

    def body(where_ref, *rest):
        d_refs = rest[:n_tensor]
        w_refs = rest[n_tensor : n_tensor + per * len(blocks)]
        out_ref = rest[-1]
        step = pl.program_id(0)
        for i in range(len(blocks)):

            @pl.when(step == i)
            def _():
                mine = w_refs[per * i : per * (i + 1)]
                w = jnp.concatenate([mine[0][...], mine[1][...]], 0)
                total = jnp.dot(d_refs[0][...], w, preferred_element_type=F32)
                for k in range(1, n_tensor):
                    total += jnp.dot(d_refs[k][...], mine[k + 1][...], preferred_element_type=F32)
                out_ref[...] = total.astype(BF16)

    fixed = lambda i, where_ref: (0, 0)

    def column(i, where_ref):
        r = blocks[-1]
        for at in range(len(blocks) - 2, -1, -1):
            r = jnp.where(i == at, blocks[at], r)
        return (0, where_ref[0] ^ r)

    operands = [d_own, *d_rest]
    specs = [pl.BlockSpec((chunk, rows), fixed)] * n_tensor
    for r in blocks:
        operands += [parts[0][r], parts[1][r]] + [others[r, k] for k in range(1, n_tensor)]
        specs += [pl.BlockSpec((half, width), fixed)] * 2 + [pl.BlockSpec((rows, width), fixed)] * (n_tensor - 1)
    aliases = {}
    if into is not None:
        operands.append(into)
        specs.append(pl.BlockSpec(memory_space=pl.ANY))
        aliases = {len(operands): 0}
    return pl.pallas_call(
        body,
        grid_spec=pltpu.PrefetchScalarGridSpec(
            num_scalar_prefetch=1,
            grid=(len(blocks),),
            in_specs=specs,
            out_specs=pl.BlockSpec((chunk, width), column),
        ),
        out_shape=jax.ShapeDtypeStruct((chunk, n_blocks * width), BF16),
        input_output_aliases=aliases,
        name="hidden_grad",
    )(where, *operands)


def add_shares(shares, where, blocks, width, into):
    chunk = shares[0].shape[0]

    def body(where_ref, *rest):
        total = rest[0][...].astype(F32)
        for ref in rest[1 : len(shares)]:
            total += ref[...].astype(F32)
        rest[-1][...] = total.astype(BF16)

    def column(i, where_ref):
        r = blocks[-1]
        for at in range(len(blocks) - 2, -1, -1):
            r = jnp.where(i == at, blocks[at], r)
        return (0, where_ref[0] ^ r)

    return pl.pallas_call(
        body,
        grid_spec=pltpu.PrefetchScalarGridSpec(
            num_scalar_prefetch=1,
            grid=(len(blocks),),
            in_specs=[pl.BlockSpec((chunk, width), lambda i, where_ref: (0, i))] * len(shares)
            + [pl.BlockSpec(memory_space=pl.ANY)],
            out_specs=pl.BlockSpec((chunk, width), column),
        ),
        out_shape=jax.ShapeDtypeStruct(into.shape, BF16),
        input_output_aliases={len(shares) + 1: 0},
        name="add_shares",
    )(where, *shares, into)


def scatter_sum(keep, sent, n_dp):
    total = keep + swap(sent, 1, n_dp).astype(F32)
    count = n_dp.bit_length() - 2
    rows, width = keep.shape[1:]
    total = total.reshape((2,) * count + (rows, width))
    half = rows // 2
    sides = []
    for at, order in ((0, list(range(count))), (half, list(range(count))[::-1])):
        part = lax.slice_in_dim(total, at, at + half, axis=count)
        left = list(range(count))[::-1]
        for b in order:
            axis = left.index(b)
            left.remove(b)
            go = lax.index_in_dim(part, 1, axis, keepdims=False).astype(BF16)
            stay = lax.index_in_dim(part, 0, axis, keepdims=False)
            part = stay + swap(go, 2 << b, n_dp).astype(F32)
        sides.append(part)
    return jnp.concatenate(sides, 0)


def local(hidden, weight, qk_scale, cotangent, n_dp, n_tensor):
    width = weight.shape[1]
    where = jnp.stack([lax.axis_index("dp"), lax.axis_index("tensor")]).astype(jnp.int32)
    parts = gather_blocks(weight, n_dp)
    others = gather_others(weight, n_tensor, n_dp)
    keys_values, d_slots, d_t = project(hidden, parts, qk_scale, cotangent, where, n_tensor)
    near = [0, 1]
    linked = sorted({r for r, k in others} - set(near))
    far = [r for r in range(n_dp) if r not in near and r not in linked]
    sent = weight_grad(d_t, hidden, where, n_dp, 1, BF16)
    share = hidden_share(d_slots, parts, far)
    keep = weight_grad(d_t, hidden, where, n_dp, 0, F32)
    d_rest = [shift(d_slots[k], k, n_tensor) for k in range(1, n_tensor)]
    shares = [share[0]] + [shift(share[k], k, n_tensor) for k in range(1, n_tensor)]
    input_grad = hidden_grad(d_slots[0], d_rest, parts, others, where, near, None)
    input_grad = hidden_grad(d_slots[0], d_rest, parts, others, where, linked, input_grad)
    input_grad = add_shares(shares, where, far, width, input_grad)
    grad = scatter_sum(keep, sent, n_dp)
    w = weight.astype(F32)
    sums = jnp.stack([jnp.sum(grad * w, 1), jnp.sum(w * w, 1), jnp.sum(grad * grad, 1)])
    bit = 1
    while bit < n_dp:
        sums = sums + swap(sums, bit, n_dp)
        bit *= 2
    gw, ww, gg = sums[0], sums[1], sums[2]
    ratio = gw / ww
    rate = step_rate * jnp.sqrt(ww / (gg + epsilon))
    norm_sq = ww + rate * rate * (gg - ratio * gw)
    scale = math.sqrt(n_dp * weight.shape[1]) / jnp.sqrt(norm_sq)
    moved = w - rate[:, None] * (grad - ratio[:, None] * w)
    new_weight = (scale[:, None] * moved).astype(BF16)
    return (keys_values, input_grad, new_weight)


def solution(mesh):
    in_specs = (P("dp", None), P("tensor", "dp"), P("tensor", None), P("dp", "tensor"))
    out_specs = (P("dp", "tensor"), P(("dp", "tensor"), None), P("tensor", "dp"))
    n_dp, n_tensor = mesh.shape["dp"], mesh.shape["tensor"]

    def body(hidden, weight, qk_scale, cotangent):
        return local(hidden, weight, qk_scale, cotangent, n_dp, n_tensor)

    return jax.shard_map(body, mesh=mesh, in_specs=in_specs, out_specs=out_specs, check_vma=False)
```

```python
import math

import jax
import jax.numpy as jnp
from jax import lax
from jax.experimental import pallas as pl
from jax.experimental.pallas import tpu as pltpu
from jax.sharding import PartitionSpec as P

step_rate = 0.5
epsilon = 1e-06
F32 = jnp.float32
BF16 = jnp.bfloat16


def swap(x, bit, n_dp):
    return lax.ppermute(x, "dp", [(i, i ^ bit) for i in range(n_dp)])


def gather_links(w, n_dp):
    bits = [1 << i for i in range(1, n_dp.bit_length() - 1)]
    half = w.shape[0] // 2
    parts = []
    for rows, order in ((w[:half], bits), (w[half:], bits[::-1])):
        have = {0: rows}
        for bit in order:
            have.update({r ^ bit: swap(x, bit, n_dp) for r, x in list(have.items())})
        parts.append(have)
    return parts


def add_core(have, n_dp):
    return {**have, **{r ^ 1: swap(x, 1, n_dp) for r, x in have.items()}}


def project(hidden, parts, qk_scale, cotangent, where, n_tensor):
    tok = hidden.shape[0]
    n_blocks = len(parts[0])
    half, width = parts[0][0].shape
    rows = 2 * half
    heads, size = qk_scale.shape
    chunk = tok // n_tensor

    def body(where_ref, h_ref, s_ref, c_ref, *rest):
        w_refs = rest[: 2 * n_blocks]
        out_ref, d_ref, dt_ref, acc = rest[2 * n_blocks :]
        step = pl.program_id(0)
        for r in range(n_blocks):

            @pl.when(step == r)
            def _():
                w = jnp.concatenate([w_refs[2 * r][...], w_refs[2 * r + 1][...]], 0)
                part = lax.dot_general(h_ref[...], w, (((1,), (1,)), ((), ())), preferred_element_type=F32)
                if r == 0:
                    acc[...] = part
                else:
                    acc[...] += part

        @pl.when(step == n_blocks - 1)
        def _():
            for h in range(heads):
                k_at = slice(2 * h * size, (2 * h + 1) * size)
                v_at = slice((2 * h + 1) * size, (2 * h + 2) * size)
                key_raw = acc[:, k_at]
                length = jnp.sqrt(jnp.sum(key_raw * key_raw, -1, keepdims=True) + epsilon)
                unit = key_raw / length
                factor = s_ref[h : h + 1, :] * math.sqrt(size)
                out_ref[:, k_at] = (factor * unit).astype(BF16)
                out_ref[:, v_at] = acc[:, v_at].astype(BF16)
                along = factor * c_ref[:, k_at].astype(F32)
                grad = (along - unit * jnp.sum(unit * along, -1, keepdims=True)) / length
                for j in range(n_tensor):
                    slot = lax.rem(where_ref[1] + (n_tensor - j), n_tensor)
                    at = slice(j * chunk, (j + 1) * chunk)
                    d_ref[slot, :, k_at] = grad[at].astype(BF16)
                    d_ref[slot, :, v_at] = c_ref[at, v_at]
                dt_ref[k_at, :] = grad.T.astype(BF16)
                dt_ref[v_at, :] = c_ref[:, v_at].astype(F32).T.astype(BF16)

    fixed = lambda i, where_ref: (0, 0)
    return pl.pallas_call(
        body,
        grid_spec=pltpu.PrefetchScalarGridSpec(
            num_scalar_prefetch=1,
            grid=(n_blocks,),
            in_specs=[
                pl.BlockSpec((tok, width), lambda i, where_ref: (0, where_ref[0] ^ i)),
                pl.BlockSpec((heads, size), fixed),
                pl.BlockSpec((tok, rows), fixed),
            ]
            + [pl.BlockSpec((half, width), fixed)] * (2 * n_blocks),
            out_specs=[
                pl.BlockSpec((tok, rows), fixed),
                pl.BlockSpec((n_tensor, chunk, rows), lambda i, where_ref: (0, 0, 0)),
                pl.BlockSpec((rows, tok), fixed),
            ],
            scratch_shapes=[pltpu.VMEM((tok, rows), F32)],
        ),
        out_shape=[
            jax.ShapeDtypeStruct((tok, rows), BF16),
            jax.ShapeDtypeStruct((n_tensor, chunk, rows), BF16),
            jax.ShapeDtypeStruct((rows, tok), BF16),
        ],
        name="project",
    )(where, hidden, qk_scale, cotangent, *[parts[s][r] for r in range(n_blocks) for s in range(2)])


def weight_grad(d_t, hidden, where, n_blocks, odd, dtype):
    rows, tok = d_t.shape
    width = hidden.shape[1] // n_blocks

    def body(where_ref, d_ref, h_ref, out_ref):
        out_ref[0] = jnp.dot(d_ref[...], h_ref[...], preferred_element_type=F32).astype(dtype)

    return pl.pallas_call(
        body,
        grid_spec=pltpu.PrefetchScalarGridSpec(
            num_scalar_prefetch=1,
            grid=(n_blocks // 2,),
            in_specs=[
                pl.BlockSpec((rows, tok), lambda i, where_ref: (0, 0)),
                pl.BlockSpec((tok, width), lambda i, where_ref: (0, where_ref[0] ^ (2 * i + odd))),
            ],
            out_specs=pl.BlockSpec((1, rows, width), lambda i, where_ref: (i, 0, 0)),
        ),
        out_shape=jax.ShapeDtypeStruct((n_blocks // 2, rows, width), dtype),
        name="weight_grad_odd" if odd else "weight_grad_even",
    )(where, d_t, hidden)


def shift(x, by, n_tensor):
    return lax.ppermute(x, "tensor", [(i, (i - by) % n_tensor) for i in range(n_tensor)])


def hidden_share(d_slots, parts, blocks):
    n_tensor, chunk, rows = d_slots.shape
    half, width = parts[0][0].shape

    def body(d_ref, *rest):
        w_refs, out_ref = rest[:-1], rest[-1]
        step = pl.program_id(0)
        d = d_ref[...].reshape(n_tensor * chunk, rows)
        for i in range(len(blocks)):

            @pl.when(step == i)
            def _():
                w = jnp.concatenate([w_refs[2 * i][...], w_refs[2 * i + 1][...]], 0)
                out = jnp.dot(d, w, preferred_element_type=F32).astype(BF16)
                out_ref[...] = out.reshape(n_tensor, chunk, width)

    return pl.pallas_call(
        body,
        grid=(len(blocks),),
        in_specs=[pl.BlockSpec(d_slots.shape, lambda i: (0, 0, 0))]
        + [pl.BlockSpec((half, width), lambda i: (0, 0))] * (2 * len(blocks)),
        out_specs=pl.BlockSpec((n_tensor, chunk, width), lambda i: (0, 0, i)),
        out_shape=jax.ShapeDtypeStruct((n_tensor, chunk, len(blocks) * width), BF16),
        name="hidden_share",
    )(d_slots, *[parts[s][r] for r in blocks for s in range(2)])


def hidden_grad(d_own, d_pair, d_mid, parts, pair, mid, where, blocks, into):
    chunk = d_own.shape[0]
    half, width = parts[0][0].shape
    n_blocks = len(parts[0])
    per = 4

    def body(where_ref, *rest):
        d_refs = rest[:3]
        w_refs = rest[3 : 3 + per * len(blocks)]
        out_ref = rest[-1]
        step = pl.program_id(0)
        for i in range(len(blocks)):

            @pl.when(step == i)
            def _():
                mine = w_refs[per * i : per * (i + 1)]
                w = jnp.concatenate([mine[0][...], mine[1][...]], 0)
                total = jnp.dot(d_refs[0][...], w, preferred_element_type=F32)
                for k in (1, 2):
                    total += jnp.dot(d_refs[k][...], mine[k + 1][...], preferred_element_type=F32)
                out_ref[...] = total.astype(BF16)

    fixed = lambda i, where_ref: (0, 0)

    def column(i, where_ref):
        r = blocks[-1]
        for at in range(len(blocks) - 2, -1, -1):
            r = jnp.where(i == at, blocks[at], r)
        return (0, where_ref[0] ^ r)

    operands = [d_own, d_pair, d_mid]
    for r in blocks:
        operands += [parts[0][r], parts[1][r], pair[r], mid[r]]
    specs = [pl.BlockSpec(x.shape, fixed) for x in operands]
    aliases = {}
    if into is not None:
        operands.append(into)
        specs.append(pl.BlockSpec(memory_space=pl.ANY))
        aliases = {len(operands): 0}
    return pl.pallas_call(
        body,
        grid_spec=pltpu.PrefetchScalarGridSpec(
            num_scalar_prefetch=1,
            grid=(len(blocks),),
            in_specs=specs,
            out_specs=pl.BlockSpec((chunk, width), column),
        ),
        out_shape=jax.ShapeDtypeStruct((chunk, n_blocks * width), BF16),
        input_output_aliases=aliases,
        name="hidden_grad",
    )(where, *operands)


def add_shares(shares, where, blocks, width, into):
    chunk = shares[0].shape[0]

    def body(where_ref, *rest):
        total = rest[0][...].astype(F32)
        for ref in rest[1 : len(shares)]:
            total += ref[...].astype(F32)
        rest[-1][...] = total.astype(BF16)

    def column(i, where_ref):
        r = blocks[-1]
        for at in range(len(blocks) - 2, -1, -1):
            r = jnp.where(i == at, blocks[at], r)
        return (0, where_ref[0] ^ r)

    return pl.pallas_call(
        body,
        grid_spec=pltpu.PrefetchScalarGridSpec(
            num_scalar_prefetch=1,
            grid=(len(blocks),),
            in_specs=[pl.BlockSpec((chunk, width), lambda i, where_ref: (0, i))] * len(shares)
            + [pl.BlockSpec(memory_space=pl.ANY)],
            out_specs=pl.BlockSpec((chunk, width), column),
        ),
        out_shape=jax.ShapeDtypeStruct(into.shape, BF16),
        input_output_aliases={len(shares) + 1: 0},
        name="add_shares",
    )(where, *shares, into)


def halve(part, axis, bit, n_dp):
    go = lax.index_in_dim(part, 1, axis, keepdims=False).astype(BF16)
    stay = lax.index_in_dim(part, 0, axis, keepdims=False)
    return stay + swap(go, bit, n_dp).astype(F32)


def local(hidden, weight, qk_scale, cotangent, n_dp, n_tensor):
    width = weight.shape[1]
    half = weight.shape[0] // 2
    where = jnp.stack([lax.axis_index("dp"), lax.axis_index("tensor")]).astype(jnp.int32)
    ahead = shift(weight, 1, n_tensor)
    behind = shift(weight, -1, n_tensor)
    parts = gather_links(weight, n_dp)
    parts, ahead, behind = lax.optimization_barrier((parts, ahead, behind))
    pair = {0: jnp.concatenate([ahead, behind], 0)}
    low, high = shift(ahead[:half], 1, n_tensor), shift(behind[half:], -1, n_tensor)
    bits = [1 << i for i in range(1, n_dp.bit_length() - 1)]
    pair.update({bit: swap(pair[0], bit, n_dp) for bit in bits})
    parts = [add_core(have, n_dp) for have in parts]
    keys_values, d_slots, d_t = project(hidden, parts, qk_scale, cotangent, where, n_tensor)
    near = [0, 1]
    linked = [r for bit in bits for r in (bit, bit ^ 1)]
    far = [r for r in range(n_dp) if r not in near and r not in linked]
    share = hidden_share(d_slots, parts, far)
    d_t, share, low, high = lax.optimization_barrier((d_t, share, low, high))
    shares = [share[0]] + [shift(share[k], k, n_tensor) for k in range(1, n_tensor)]
    mid = {0: jnp.concatenate([low, high], 0)}
    mid.update({bit: swap(mid[0], bit, n_dp) for bit in bits})
    sent = weight_grad(d_t, hidden, where, n_dp, 1, BF16)
    d_rest = [shift(d_slots[k], k, n_tensor) for k in range(1, n_tensor)]
    d_t, sent, pair, d_rest = lax.optimization_barrier((d_t, sent, pair, d_rest))
    pair = add_core(pair, n_dp)
    keep = weight_grad(d_t, hidden, where, n_dp, 0, F32)
    total = keep + swap(sent, 1, n_dp).astype(F32)
    total, mid_links = lax.optimization_barrier((total, mid))
    mid = add_core(mid_links, n_dp)
    count = len(bits)
    total = total.reshape((2,) * count + total.shape[1:])
    sides = [total[..., :half, :], total[..., half:, :]]
    orders = [list(range(count)), list(range(count))[::-1]]
    left = [list(range(count))[::-1], list(range(count))[::-1]]
    for step in range(count):
        if step == count - 1:
            sides, shares[1], shares[-1] = lax.optimization_barrier((sides, shares[1], shares[-1]))
        for at in range(2):
            b = orders[at][step]
            axis = left[at].index(b)
            left[at].remove(b)
            sides[at] = halve(sides[at], axis, bits[b], n_dp)
    grad = jnp.concatenate(sides, 0)
    grad, shares[2] = lax.optimization_barrier((grad, shares[2]))
    d_pair = jnp.concatenate([d_rest[0], d_rest[-1]], 1)
    d_all = (d_slots[0], d_pair, d_rest[1], parts, pair, mid, where)
    input_grad = hidden_grad(*d_all, near, None)
    input_grad = hidden_grad(*d_all, linked, input_grad)
    input_grad = add_shares(shares, where, far, width, input_grad)
    w = weight.astype(F32)
    sums = jnp.stack([jnp.sum(grad * w, 1), jnp.sum(w * w, 1), jnp.sum(grad * grad, 1)])
    bit = 1
    while bit < n_dp:
        sums = sums + swap(sums, bit, n_dp)
        bit *= 2
    gw, ww, gg = sums[0], sums[1], sums[2]
    ratio = gw / ww
    rate = step_rate * jnp.sqrt(ww / (gg + epsilon))
    norm_sq = ww + rate * rate * (gg - ratio * gw)
    scale = math.sqrt(n_dp * weight.shape[1]) / jnp.sqrt(norm_sq)
    moved = w - rate[:, None] * (grad - ratio[:, None] * w)
    new_weight = (scale[:, None] * moved).astype(BF16)
    return (keys_values, input_grad, new_weight)


def solution(mesh):
    in_specs = (P("dp", None), P("tensor", "dp"), P("tensor", None), P("dp", "tensor"))
    out_specs = (P("dp", "tensor"), P(("dp", "tensor"), None), P("tensor", "dp"))
    n_dp, n_tensor = mesh.shape["dp"], mesh.shape["tensor"]

    def body(hidden, weight, qk_scale, cotangent):
        return local(hidden, weight, qk_scale, cotangent, n_dp, n_tensor)

    return jax.shard_map(body, mesh=mesh, in_specs=in_specs, out_specs=out_specs, check_vma=False)
```

```python
import math

import jax
import jax.numpy as jnp
from jax import lax
from jax.experimental import pallas as pl
from jax.experimental.pallas import tpu as pltpu
from jax.sharding import PartitionSpec as P

step_rate = 0.5
epsilon = 1e-06
F32 = jnp.float32
BF16 = jnp.bfloat16


def swap(x, bit, n_dp):
    return lax.ppermute(x, "dp", [(i, i ^ bit) for i in range(n_dp)])


def gather_links(w, n_dp):
    bits = [1 << i for i in range(1, n_dp.bit_length() - 1)]
    half = w.shape[0] // 2
    parts = []
    for rows, order in ((w[:half], bits), (w[half:], bits[::-1])):
        have = {0: rows}
        for bit in order:
            have.update({r ^ bit: swap(x, bit, n_dp) for r, x in list(have.items())})
        parts.append(have)
    return parts


def add_core(have, n_dp):
    return {**have, **{r ^ 1: swap(x, 1, n_dp) for r, x in have.items()}}


def project(hidden, parts, qk_scale, cotangent, where, n_tensor):
    tok = hidden.shape[0]
    n_blocks = len(parts[0])
    half, width = parts[0][0].shape
    rows = 2 * half
    heads, size = qk_scale.shape
    chunk = tok // n_tensor

    def body(where_ref, h_ref, s_ref, c_ref, *rest):
        w_refs = rest[: 2 * n_blocks]
        out_ref, d_ref, dt_ref, acc = rest[2 * n_blocks :]
        step = pl.program_id(0)
        for r in range(n_blocks):

            @pl.when(step == r)
            def _():
                w = jnp.concatenate([w_refs[2 * r][...], w_refs[2 * r + 1][...]], 0)
                part = lax.dot_general(h_ref[...], w, (((1,), (1,)), ((), ())), preferred_element_type=F32)
                if r == 0:
                    acc[...] = part
                else:
                    acc[...] += part

        @pl.when(step == n_blocks - 1)
        def _():
            for h in range(heads):
                k_at = slice(2 * h * size, (2 * h + 1) * size)
                v_at = slice((2 * h + 1) * size, (2 * h + 2) * size)
                key_raw = acc[:, k_at]
                length = jnp.sqrt(jnp.sum(key_raw * key_raw, -1, keepdims=True) + epsilon)
                unit = key_raw / length
                factor = s_ref[h : h + 1, :] * math.sqrt(size)
                out_ref[:, k_at] = (factor * unit).astype(BF16)
                out_ref[:, v_at] = acc[:, v_at].astype(BF16)
                along = factor * c_ref[:, k_at].astype(F32)
                grad = (along - unit * jnp.sum(unit * along, -1, keepdims=True)) / length
                for j in range(n_tensor):
                    slot = lax.rem(where_ref[1] + (n_tensor - j), n_tensor)
                    at = slice(j * chunk, (j + 1) * chunk)
                    d_ref[slot, :, k_at] = grad[at].astype(BF16)
                    d_ref[slot, :, v_at] = c_ref[at, v_at]
                dt_ref[k_at, :] = grad.T.astype(BF16)
                dt_ref[v_at, :] = c_ref[:, v_at].astype(F32).T.astype(BF16)

    fixed = lambda i, where_ref: (0, 0)
    return pl.pallas_call(
        body,
        grid_spec=pltpu.PrefetchScalarGridSpec(
            num_scalar_prefetch=1,
            grid=(n_blocks,),
            in_specs=[
                pl.BlockSpec((tok, width), lambda i, where_ref: (0, where_ref[0] ^ i)),
                pl.BlockSpec((heads, size), fixed),
                pl.BlockSpec((tok, rows), fixed),
            ]
            + [pl.BlockSpec((half, width), fixed)] * (2 * n_blocks),
            out_specs=[
                pl.BlockSpec((tok, rows), fixed),
                pl.BlockSpec((n_tensor, chunk, rows), lambda i, where_ref: (0, 0, 0)),
                pl.BlockSpec((rows, tok), fixed),
            ],
            scratch_shapes=[pltpu.VMEM((tok, rows), F32)],
        ),
        out_shape=[
            jax.ShapeDtypeStruct((tok, rows), BF16),
            jax.ShapeDtypeStruct((n_tensor, chunk, rows), BF16),
            jax.ShapeDtypeStruct((rows, tok), BF16),
        ],
        name="project",
    )(where, hidden, qk_scale, cotangent, *[parts[s][r] for r in range(n_blocks) for s in range(2)])


def weight_grad(d_t, hidden, where, n_blocks, odd, dtype):
    rows, tok = d_t.shape
    width = hidden.shape[1] // n_blocks

    def body(where_ref, d_ref, h_ref, out_ref):
        out_ref[0] = jnp.dot(d_ref[...], h_ref[...], preferred_element_type=F32).astype(dtype)

    return pl.pallas_call(
        body,
        grid_spec=pltpu.PrefetchScalarGridSpec(
            num_scalar_prefetch=1,
            grid=(n_blocks // 2,),
            in_specs=[
                pl.BlockSpec((rows, tok), lambda i, where_ref: (0, 0)),
                pl.BlockSpec((tok, width), lambda i, where_ref: (0, where_ref[0] ^ (2 * i + odd))),
            ],
            out_specs=pl.BlockSpec((1, rows, width), lambda i, where_ref: (i, 0, 0)),
        ),
        out_shape=jax.ShapeDtypeStruct((n_blocks // 2, rows, width), dtype),
        name="weight_grad_odd" if odd else "weight_grad_even",
    )(where, d_t, hidden)


def shift(x, by, n_tensor):
    return lax.ppermute(x, "tensor", [(i, (i - by) % n_tensor) for i in range(n_tensor)])


def hidden_share(d_slots, parts, blocks):
    n_tensor, chunk, rows = d_slots.shape
    half, width = parts[0][0].shape

    def body(d_ref, *rest):
        w_refs, out_ref = rest[:-1], rest[-1]
        step = pl.program_id(0)
        d = d_ref[...].reshape(n_tensor * chunk, rows)
        for i in range(len(blocks)):

            @pl.when(step == i)
            def _():
                w = jnp.concatenate([w_refs[2 * i][...], w_refs[2 * i + 1][...]], 0)
                out = jnp.dot(d, w, preferred_element_type=F32).astype(BF16)
                out_ref[...] = out.reshape(n_tensor, chunk, width)

    return pl.pallas_call(
        body,
        grid=(len(blocks),),
        in_specs=[pl.BlockSpec(d_slots.shape, lambda i: (0, 0, 0))]
        + [pl.BlockSpec((half, width), lambda i: (0, 0))] * (2 * len(blocks)),
        out_specs=pl.BlockSpec((n_tensor, chunk, width), lambda i: (0, 0, i)),
        out_shape=jax.ShapeDtypeStruct((n_tensor, chunk, len(blocks) * width), BF16),
        name="hidden_share",
    )(d_slots, *[parts[s][r] for r in blocks for s in range(2)])


def hidden_grad(d_own, d_pair, d_mid, parts, pair, mid, where, blocks, into):
    chunk = d_own.shape[0]
    half, width = parts[0][0].shape
    n_blocks = len(parts[0])
    per = 4

    def body(where_ref, *rest):
        d_refs = rest[:3]
        w_refs = rest[3 : 3 + per * len(blocks)]
        out_ref = rest[-1]
        step = pl.program_id(0)
        for i in range(len(blocks)):

            @pl.when(step == i)
            def _():
                mine = w_refs[per * i : per * (i + 1)]
                w = jnp.concatenate([mine[0][...], mine[1][...]], 0)
                total = jnp.dot(d_refs[0][...], w, preferred_element_type=F32)
                for k in (1, 2):
                    total += jnp.dot(d_refs[k][...], mine[k + 1][...], preferred_element_type=F32)
                out_ref[...] = total.astype(BF16)

    fixed = lambda i, where_ref: (0, 0)

    def column(i, where_ref):
        r = blocks[-1]
        for at in range(len(blocks) - 2, -1, -1):
            r = jnp.where(i == at, blocks[at], r)
        return (0, where_ref[0] ^ r)

    operands = [d_own, d_pair, d_mid]
    for r in blocks:
        operands += [parts[0][r], parts[1][r], pair[r], mid[r]]
    specs = [pl.BlockSpec(x.shape, fixed) for x in operands]
    aliases = {}
    if into is not None:
        operands.append(into)
        specs.append(pl.BlockSpec(memory_space=pl.ANY))
        aliases = {len(operands): 0}
    return pl.pallas_call(
        body,
        grid_spec=pltpu.PrefetchScalarGridSpec(
            num_scalar_prefetch=1,
            grid=(len(blocks),),
            in_specs=specs,
            out_specs=pl.BlockSpec((chunk, width), column),
        ),
        out_shape=jax.ShapeDtypeStruct((chunk, n_blocks * width), BF16),
        input_output_aliases=aliases,
        name="hidden_grad",
    )(where, *operands)


def add_shares(shares, where, blocks, width, into):
    chunk = shares[0].shape[0]

    def body(where_ref, *rest):
        total = rest[0][...].astype(F32)
        for ref in rest[1 : len(shares)]:
            total += ref[...].astype(F32)
        rest[-1][...] = total.astype(BF16)

    def column(i, where_ref):
        r = blocks[-1]
        for at in range(len(blocks) - 2, -1, -1):
            r = jnp.where(i == at, blocks[at], r)
        return (0, where_ref[0] ^ r)

    return pl.pallas_call(
        body,
        grid_spec=pltpu.PrefetchScalarGridSpec(
            num_scalar_prefetch=1,
            grid=(len(blocks),),
            in_specs=[pl.BlockSpec((chunk, width), lambda i, where_ref: (0, i))] * len(shares)
            + [pl.BlockSpec(memory_space=pl.ANY)],
            out_specs=pl.BlockSpec((chunk, width), column),
        ),
        out_shape=jax.ShapeDtypeStruct(into.shape, BF16),
        input_output_aliases={len(shares) + 1: 0},
        name="add_shares",
    )(where, *shares, into)


def halve(part, axis, bit, n_dp):
    go = lax.index_in_dim(part, 1, axis, keepdims=False).astype(BF16)
    stay = lax.index_in_dim(part, 0, axis, keepdims=False)
    return stay + swap(go, bit, n_dp).astype(F32)


def local(hidden, weight, qk_scale, cotangent, n_dp, n_tensor):
    width = weight.shape[1]
    half = weight.shape[0] // 2
    where = jnp.stack([lax.axis_index("dp"), lax.axis_index("tensor")]).astype(jnp.int32)
    ahead = shift(weight, 1, n_tensor)
    behind = shift(weight, -1, n_tensor)
    parts = [add_core(have, n_dp) for have in gather_links(weight, n_dp)]
    parts, ahead, behind = lax.optimization_barrier((parts, ahead, behind))
    pair = {0: jnp.concatenate([ahead, behind], 0)}
    low, high = shift(ahead[:half], 1, n_tensor), shift(behind[half:], -1, n_tensor)
    bits = [1 << i for i in range(1, n_dp.bit_length() - 1)]
    pair.update({bit: swap(pair[0], bit, n_dp) for bit in bits})
    keys_values, d_slots, d_t = project(hidden, parts, qk_scale, cotangent, where, n_tensor)
    near = [0, 1]
    linked = [r for bit in bits for r in (bit, bit ^ 1)]
    far = [r for r in range(n_dp) if r not in near and r not in linked]
    share = hidden_share(d_slots, parts, far)
    d_t, share, low, high = lax.optimization_barrier((d_t, share, low, high))
    cut = share.shape[2] // 2
    via_ahead = shift(share[2, :, :cut], 1, n_tensor)
    via_behind = shift(share[2, :, cut:], -1, n_tensor)
    mid = {0: jnp.concatenate([low, high], 0)}
    mid.update({bit: swap(mid[0], bit, n_dp) for bit in bits})
    sent = weight_grad(d_t, hidden, where, n_dp, 1, BF16)
    d_rest = [shift(d_slots[k], k, n_tensor) for k in range(1, n_tensor)]
    due = (d_t, sent, pair, d_rest, via_ahead, via_behind)
    d_t, sent, pair, d_rest, via_ahead, via_behind = lax.optimization_barrier(due)
    to_ahead = jnp.concatenate([share[1, :, :cut] + via_ahead, share[1, :, cut:]], 1)
    to_behind = jnp.concatenate([share[-1, :, :cut], share[-1, :, cut:] + via_behind], 1)
    from_ahead, from_behind = shift(to_ahead, 1, n_tensor), shift(to_behind, -1, n_tensor)
    pair = add_core(pair, n_dp)
    keep = weight_grad(d_t, hidden, where, n_dp, 0, F32)
    total = keep + swap(sent, 1, n_dp).astype(F32)
    total, mid, from_ahead, from_behind = lax.optimization_barrier((total, mid, from_ahead, from_behind))
    mid = add_core(mid, n_dp)
    d_pair = jnp.concatenate([d_rest[0], d_rest[-1]], 1)
    d_all = (d_slots[0], d_pair, d_rest[1], parts, pair, mid, where)
    input_grad = hidden_grad(*d_all, near, None)
    count = len(bits)
    total = total.reshape((2,) * count + total.shape[1:])
    sides = [total[..., :half, :], total[..., half:, :]]
    orders = [list(range(count)), list(range(count))[::-1]]
    left = [list(range(count))[::-1], list(range(count))[::-1]]
    for step in range(count):
        if step == count - 1:
            sides, input_grad = lax.optimization_barrier((sides, input_grad))
        for at in range(2):
            b = orders[at][step]
            axis = left[at].index(b)
            left[at].remove(b)
            sides[at] = halve(sides[at], axis, bits[b], n_dp)
    input_grad = hidden_grad(*d_all, linked, input_grad)
    sides, input_grad = lax.optimization_barrier((sides, input_grad))
    grad = jnp.concatenate(sides, 0)
    input_grad = add_shares([share[0], from_ahead, from_behind], where, far, width, input_grad)
    w = weight.astype(F32)
    sums = jnp.stack([jnp.sum(grad * w, 1), jnp.sum(w * w, 1), jnp.sum(grad * grad, 1)])
    bit = 1
    while bit < n_dp:
        sums = sums + swap(sums, bit, n_dp)
        bit *= 2
    gw, ww, gg = sums[0], sums[1], sums[2]
    ratio = gw / ww
    rate = step_rate * jnp.sqrt(ww / (gg + epsilon))
    norm_sq = ww + rate * rate * (gg - ratio * gw)
    scale = math.sqrt(n_dp * weight.shape[1]) / jnp.sqrt(norm_sq)
    moved = w - rate[:, None] * (grad - ratio[:, None] * w)
    new_weight = (scale[:, None] * moved).astype(BF16)
    return (keys_values, input_grad, new_weight)


def solution(mesh):
    in_specs = (P("dp", None), P("tensor", "dp"), P("tensor", None), P("dp", "tensor"))
    out_specs = (P("dp", "tensor"), P(("dp", "tensor"), None), P("tensor", "dp"))
    n_dp, n_tensor = mesh.shape["dp"], mesh.shape["tensor"]

    def body(hidden, weight, qk_scale, cotangent):
        return local(hidden, weight, qk_scale, cotangent, n_dp, n_tensor)

    return jax.shard_map(body, mesh=mesh, in_specs=in_specs, out_specs=out_specs, check_vma=False)
```

```python
import math

import jax
import jax.numpy as jnp
from jax import lax
from jax.experimental import pallas as pl
from jax.experimental.pallas import tpu as pltpu
from jax.sharding import PartitionSpec as P

step_rate = 0.5
epsilon = 1e-06
F32 = jnp.float32
BF16 = jnp.bfloat16


def swap(x, bit, n_dp):
    return lax.ppermute(x, "dp", [(i, i ^ bit) for i in range(n_dp)])


def gather_links(w, n_dp):
    bits = [1 << i for i in range(1, n_dp.bit_length() - 1)]
    half = w.shape[0] // 2
    parts = []
    for rows, order in ((w[:half], bits), (w[half:], bits[::-1])):
        have = {0: rows}
        for bit in order:
            have.update({r ^ bit: swap(x, bit, n_dp) for r, x in list(have.items())})
        parts.append(have)
    return parts


def add_core(have, n_dp):
    return {**have, **{r ^ 1: swap(x, 1, n_dp) for r, x in have.items()}}


def project(hidden, parts, qk_scale, cotangent, where, n_tensor):
    tok = hidden.shape[0]
    n_blocks = len(parts[0])
    half, width = parts[0][0].shape
    rows = 2 * half
    heads, size = qk_scale.shape
    chunk = tok // n_tensor

    def body(where_ref, h_ref, s_ref, c_ref, *rest):
        w_refs = rest[: 2 * n_blocks]
        out_ref, d_ref, dt_ref, acc = rest[2 * n_blocks :]
        step = pl.program_id(0)
        for r in range(n_blocks):

            @pl.when(step == r)
            def _():
                w = jnp.concatenate([w_refs[2 * r][...], w_refs[2 * r + 1][...]], 0)
                part = lax.dot_general(h_ref[...], w, (((1,), (1,)), ((), ())), preferred_element_type=F32)
                if r == 0:
                    acc[...] = part
                else:
                    acc[...] += part

        @pl.when(step == n_blocks - 1)
        def _():
            for h in range(heads):
                k_at = slice(2 * h * size, (2 * h + 1) * size)
                v_at = slice((2 * h + 1) * size, (2 * h + 2) * size)
                key_raw = acc[:, k_at]
                length = jnp.sqrt(jnp.sum(key_raw * key_raw, -1, keepdims=True) + epsilon)
                unit = key_raw / length
                factor = s_ref[h : h + 1, :] * math.sqrt(size)
                out_ref[:, k_at] = (factor * unit).astype(BF16)
                out_ref[:, v_at] = acc[:, v_at].astype(BF16)
                along = factor * c_ref[:, k_at].astype(F32)
                grad = (along - unit * jnp.sum(unit * along, -1, keepdims=True)) / length
                for j in range(n_tensor):
                    slot = lax.rem(where_ref[1] + (n_tensor - j), n_tensor)
                    at = slice(j * chunk, (j + 1) * chunk)
                    d_ref[slot, :, k_at] = grad[at].astype(BF16)
                    d_ref[slot, :, v_at] = c_ref[at, v_at]
                dt_ref[k_at, :] = grad.T.astype(BF16)
                dt_ref[v_at, :] = c_ref[:, v_at].astype(F32).T.astype(BF16)

    fixed = lambda i, where_ref: (0, 0)
    return pl.pallas_call(
        body,
        grid_spec=pltpu.PrefetchScalarGridSpec(
            num_scalar_prefetch=1,
            grid=(n_blocks,),
            in_specs=[
                pl.BlockSpec((tok, width), lambda i, where_ref: (0, where_ref[0] ^ i)),
                pl.BlockSpec((heads, size), fixed),
                pl.BlockSpec((tok, rows), fixed),
            ]
            + [pl.BlockSpec((half, width), fixed)] * (2 * n_blocks),
            out_specs=[
                pl.BlockSpec((tok, rows), fixed),
                pl.BlockSpec((n_tensor, chunk, rows), lambda i, where_ref: (0, 0, 0)),
                pl.BlockSpec((rows, tok), fixed),
            ],
            scratch_shapes=[pltpu.VMEM((tok, rows), F32)],
        ),
        out_shape=[
            jax.ShapeDtypeStruct((tok, rows), BF16),
            jax.ShapeDtypeStruct((n_tensor, chunk, rows), BF16),
            jax.ShapeDtypeStruct((rows, tok), BF16),
        ],
        name="project",
    )(where, hidden, qk_scale, cotangent, *[parts[s][r] for r in range(n_blocks) for s in range(2)])


def weight_grad(d_t, hidden, where, n_blocks, odd, dtype):
    rows, tok = d_t.shape
    width = hidden.shape[1] // n_blocks

    def body(where_ref, d_ref, h_ref, out_ref):
        out_ref[0] = jnp.dot(d_ref[...], h_ref[...], preferred_element_type=F32).astype(dtype)

    return pl.pallas_call(
        body,
        grid_spec=pltpu.PrefetchScalarGridSpec(
            num_scalar_prefetch=1,
            grid=(n_blocks // 2,),
            in_specs=[
                pl.BlockSpec((rows, tok), lambda i, where_ref: (0, 0)),
                pl.BlockSpec((tok, width), lambda i, where_ref: (0, where_ref[0] ^ (2 * i + odd))),
            ],
            out_specs=pl.BlockSpec((1, rows, width), lambda i, where_ref: (i, 0, 0)),
        ),
        out_shape=jax.ShapeDtypeStruct((n_blocks // 2, rows, width), dtype),
        name="weight_grad_odd" if odd else "weight_grad_even",
    )(where, d_t, hidden)


def shift(x, by, n_tensor):
    return lax.ppermute(x, "tensor", [(i, (i - by) % n_tensor) for i in range(n_tensor)])


def hidden_share(d_slots, parts, blocks):
    n_tensor, chunk, rows = d_slots.shape
    half, width = parts[0][0].shape

    def body(d_ref, *rest):
        w_refs, out_ref = rest[:-1], rest[-1]
        step = pl.program_id(0)
        d = d_ref[...].reshape(n_tensor * chunk, rows)
        for i in range(len(blocks)):

            @pl.when(step == i)
            def _():
                w = jnp.concatenate([w_refs[2 * i][...], w_refs[2 * i + 1][...]], 0)
                out = jnp.dot(d, w, preferred_element_type=F32).astype(BF16)
                out_ref[...] = out.reshape(n_tensor, chunk, width)

    return pl.pallas_call(
        body,
        grid=(len(blocks),),
        in_specs=[pl.BlockSpec(d_slots.shape, lambda i: (0, 0, 0))]
        + [pl.BlockSpec((half, width), lambda i: (0, 0))] * (2 * len(blocks)),
        out_specs=pl.BlockSpec((n_tensor, chunk, width), lambda i: (0, 0, i)),
        out_shape=jax.ShapeDtypeStruct((n_tensor, chunk, len(blocks) * width), BF16),
        name="hidden_share",
    )(d_slots, *[parts[s][r] for r in blocks for s in range(2)])


def hidden_grad(d_own, d_pair, d_mid, parts, pair, mid, where, blocks, into):
    chunk = d_own.shape[0]
    half, width = parts[0][0].shape
    n_blocks = len(parts[0])
    per = 4

    def body(where_ref, *rest):
        d_refs = rest[:3]
        w_refs = rest[3 : 3 + per * len(blocks)]
        out_ref = rest[-1]
        step = pl.program_id(0)
        for i in range(len(blocks)):

            @pl.when(step == i)
            def _():
                mine = w_refs[per * i : per * (i + 1)]
                w = jnp.concatenate([mine[0][...], mine[1][...]], 0)
                total = jnp.dot(d_refs[0][...], w, preferred_element_type=F32)
                for k in (1, 2):
                    total += jnp.dot(d_refs[k][...], mine[k + 1][...], preferred_element_type=F32)
                out_ref[...] = total.astype(BF16)

    fixed = lambda i, where_ref: (0, 0)

    def column(i, where_ref):
        r = blocks[-1]
        for at in range(len(blocks) - 2, -1, -1):
            r = jnp.where(i == at, blocks[at], r)
        return (0, where_ref[0] ^ r)

    operands = [d_own, d_pair, d_mid]
    for r in blocks:
        operands += [parts[0][r], parts[1][r], pair[r], mid[r]]
    specs = [pl.BlockSpec(x.shape, fixed) for x in operands]
    aliases = {}
    if into is not None:
        operands.append(into)
        specs.append(pl.BlockSpec(memory_space=pl.ANY))
        aliases = {len(operands): 0}
    return pl.pallas_call(
        body,
        grid_spec=pltpu.PrefetchScalarGridSpec(
            num_scalar_prefetch=1,
            grid=(len(blocks),),
            in_specs=specs,
            out_specs=pl.BlockSpec((chunk, width), column),
        ),
        out_shape=jax.ShapeDtypeStruct((chunk, n_blocks * width), BF16),
        input_output_aliases=aliases,
        name="hidden_grad",
    )(where, *operands)


def add_shares(shares, where, blocks, width, into):
    chunk = shares[0].shape[0]

    def body(where_ref, *rest):
        total = rest[0][...].astype(F32)
        for ref in rest[1 : len(shares)]:
            total += ref[...].astype(F32)
        rest[-1][...] = total.astype(BF16)

    def column(i, where_ref):
        r = blocks[-1]
        for at in range(len(blocks) - 2, -1, -1):
            r = jnp.where(i == at, blocks[at], r)
        return (0, where_ref[0] ^ r)

    return pl.pallas_call(
        body,
        grid_spec=pltpu.PrefetchScalarGridSpec(
            num_scalar_prefetch=1,
            grid=(len(blocks),),
            in_specs=[pl.BlockSpec((chunk, width), lambda i, where_ref: (0, i))] * len(shares)
            + [pl.BlockSpec(memory_space=pl.ANY)],
            out_specs=pl.BlockSpec((chunk, width), column),
        ),
        out_shape=jax.ShapeDtypeStruct(into.shape, BF16),
        input_output_aliases={len(shares) + 1: 0},
        name="add_shares",
    )(where, *shares, into)


def halve(part, axis, bit, n_dp):
    go = lax.index_in_dim(part, 1, axis, keepdims=False).astype(BF16)
    stay = lax.index_in_dim(part, 0, axis, keepdims=False)
    return stay + swap(go, bit, n_dp).astype(F32)


def local(hidden, weight, qk_scale, cotangent, n_dp, n_tensor):
    width = weight.shape[1]
    half = weight.shape[0] // 2
    where = jnp.stack([lax.axis_index("dp"), lax.axis_index("tensor")]).astype(jnp.int32)
    ahead = shift(weight, 1, n_tensor)
    behind = shift(weight, -1, n_tensor)
    parts = gather_links(weight, n_dp)
    last = n_dp - 2
    final = [have[last] for have in parts]
    parts = [add_core({r: x for r, x in have.items() if r != last}, n_dp) for have in parts]
    final, ahead, behind = lax.optimization_barrier((final, ahead, behind))
    for have, x in zip(parts, final):
        have.update(add_core({last: x}, n_dp))
    pair = {0: jnp.concatenate([ahead, behind], 0)}
    across = shift(weight, 2, n_tensor)
    bits = [1 << i for i in range(1, n_dp.bit_length() - 1)]
    pair.update({bit: swap(pair[0], bit, n_dp) for bit in bits})
    keys_values, d_slots, d_t = project(hidden, parts, qk_scale, cotangent, where, n_tensor)
    near = [0, 1]
    linked = [r for bit in bits for r in (bit, bit ^ 1)]
    far = [r for r in range(n_dp) if r not in near and r not in linked]
    share = hidden_share(d_slots, parts, far)
    d_rest = [shift(d_slots[k], k, n_tensor) for k in range(1, n_tensor)]
    d_t, share, across, d_rest = lax.optimization_barrier((d_t, share, across, d_rest))
    cut = share.shape[2] // 2
    via_ahead = shift(share[2, :, :cut], 1, n_tensor)
    via_behind = shift(share[2, :, cut:], -1, n_tensor)
    mid = {0: across}
    mid.update({bit: swap(mid[0], bit, n_dp) for bit in bits})
    sent = weight_grad(d_t, hidden, where, n_dp, 1, BF16)
    due = (d_t, sent, pair, via_ahead, via_behind)
    d_t, sent, pair, via_ahead, via_behind = lax.optimization_barrier(due)
    to_ahead = jnp.concatenate([share[1, :, :cut] + via_ahead, share[1, :, cut:]], 1)
    to_behind = jnp.concatenate([share[-1, :, :cut], share[-1, :, cut:] + via_behind], 1)
    from_ahead, from_behind = shift(to_ahead, 1, n_tensor), shift(to_behind, -1, n_tensor)
    pair = add_core(pair, n_dp)
    keep = weight_grad(d_t, hidden, where, n_dp, 0, F32)
    total = keep + swap(sent, 1, n_dp).astype(F32)
    total, mid = lax.optimization_barrier((total, mid))
    mid = add_core(mid, n_dp)
    d_pair = jnp.concatenate([d_rest[0], d_rest[-1]], 1)
    d_all = (d_slots[0], d_pair, d_rest[1], parts, pair, mid, where)
    input_grad = hidden_grad(*d_all, near, None)
    count = len(bits)
    total = total.reshape((2,) * count + total.shape[1:])
    sides = [total[..., :half, :], total[..., half:, :]]
    orders = [list(range(count)), list(range(count))[::-1]]
    left = [list(range(count))[::-1], list(range(count))[::-1]]
    for step in range(count):
        if step == count - 1:
            due = (sides, input_grad, from_ahead, from_behind)
            sides, input_grad, from_ahead, from_behind = lax.optimization_barrier(due)
        for at in range(2):
            b = orders[at][step]
            axis = left[at].index(b)
            left[at].remove(b)
            sides[at] = halve(sides[at], axis, bits[b], n_dp)
    input_grad = hidden_grad(*d_all, linked, input_grad)
    sides, input_grad = lax.optimization_barrier((sides, input_grad))
    grad = jnp.concatenate(sides, 0)
    input_grad = add_shares([share[0], from_ahead, from_behind], where, far, width, input_grad)
    w = weight.astype(F32)
    sums = jnp.stack([jnp.sum(grad * w, 1), jnp.sum(w * w, 1), jnp.sum(grad * grad, 1)])
    bit = 1
    while bit < n_dp:
        sums = sums + swap(sums, bit, n_dp)
        bit *= 2
    gw, ww, gg = sums[0], sums[1], sums[2]
    ratio = gw / ww
    rate = step_rate * jnp.sqrt(ww / (gg + epsilon))
    norm_sq = ww + rate * rate * (gg - ratio * gw)
    scale = math.sqrt(n_dp * weight.shape[1]) / jnp.sqrt(norm_sq)
    moved = w - rate[:, None] * (grad - ratio[:, None] * w)
    new_weight = (scale[:, None] * moved).astype(BF16)
    return (keys_values, input_grad, new_weight)


def solution(mesh):
    in_specs = (P("dp", None), P("tensor", "dp"), P("tensor", None), P("dp", "tensor"))
    out_specs = (P("dp", "tensor"), P(("dp", "tensor"), None), P("tensor", "dp"))
    n_dp, n_tensor = mesh.shape["dp"], mesh.shape["tensor"]

    def body(hidden, weight, qk_scale, cotangent):
        return local(hidden, weight, qk_scale, cotangent, n_dp, n_tensor)

    return jax.shard_map(body, mesh=mesh, in_specs=in_specs, out_specs=out_specs, check_vma=False)
```

```python
import math

import jax
import jax.numpy as jnp
from jax import lax
from jax.experimental import pallas as pl
from jax.experimental.pallas import tpu as pltpu
from jax.sharding import PartitionSpec as P

step_rate = 0.5
epsilon = 1e-06
F32 = jnp.float32
BF16 = jnp.bfloat16


def swap(x, bit, n_dp):
    return lax.ppermute(x, "dp", [(i, i ^ bit) for i in range(n_dp)])


def gather_links(w, n_dp):
    bits = [1 << i for i in range(1, n_dp.bit_length() - 1)]
    half = w.shape[0] // 2
    parts = []
    for rows, order in ((w[:half], bits), (w[half:], bits[::-1])):
        have = {0: rows}
        for bit in order:
            have.update({r ^ bit: swap(x, bit, n_dp) for r, x in list(have.items())})
        parts.append(have)
    return parts


def add_core(have, n_dp):
    return {**have, **{r ^ 1: swap(x, 1, n_dp) for r, x in have.items()}}


def project(hidden, parts, qk_scale, cotangent, where, n_tensor):
    tok = hidden.shape[0]
    n_blocks = len(parts[0])
    half, width = parts[0][0].shape
    rows = 2 * half
    heads, size = qk_scale.shape
    chunk = tok // n_tensor

    def body(where_ref, h_ref, s_ref, c_ref, *rest):
        w_refs = rest[: 2 * n_blocks]
        out_ref, d_ref, dt_ref, acc = rest[2 * n_blocks :]
        step = pl.program_id(0)
        for r in range(n_blocks):

            @pl.when(step == r)
            def _():
                w = jnp.concatenate([w_refs[2 * r][...], w_refs[2 * r + 1][...]], 0)
                part = lax.dot_general(h_ref[...], w, (((1,), (1,)), ((), ())), preferred_element_type=F32)
                if r == 0:
                    acc[...] = part
                else:
                    acc[...] += part

        @pl.when(step == n_blocks - 1)
        def _():
            for h in range(heads):
                k_at = slice(2 * h * size, (2 * h + 1) * size)
                v_at = slice((2 * h + 1) * size, (2 * h + 2) * size)
                key_raw = acc[:, k_at]
                length = jnp.sqrt(jnp.sum(key_raw * key_raw, -1, keepdims=True) + epsilon)
                unit = key_raw / length
                factor = s_ref[h : h + 1, :] * math.sqrt(size)
                out_ref[:, k_at] = (factor * unit).astype(BF16)
                out_ref[:, v_at] = acc[:, v_at].astype(BF16)
                along = factor * c_ref[:, k_at].astype(F32)
                grad = (along - unit * jnp.sum(unit * along, -1, keepdims=True)) / length
                for j in range(n_tensor):
                    slot = lax.rem(where_ref[1] + (n_tensor - j), n_tensor)
                    at = slice(j * chunk, (j + 1) * chunk)
                    d_ref[slot, :, k_at] = grad[at].astype(BF16)
                    d_ref[slot, :, v_at] = c_ref[at, v_at]
                dt_ref[k_at, :] = grad.T.astype(BF16)
                dt_ref[v_at, :] = c_ref[:, v_at].astype(F32).T.astype(BF16)

    fixed = lambda i, where_ref: (0, 0)
    return pl.pallas_call(
        body,
        grid_spec=pltpu.PrefetchScalarGridSpec(
            num_scalar_prefetch=1,
            grid=(n_blocks,),
            in_specs=[
                pl.BlockSpec((tok, width), lambda i, where_ref: (0, where_ref[0] ^ i)),
                pl.BlockSpec((heads, size), fixed),
                pl.BlockSpec((tok, rows), fixed),
            ]
            + [pl.BlockSpec((half, width), fixed)] * (2 * n_blocks),
            out_specs=[
                pl.BlockSpec((tok, rows), fixed),
                pl.BlockSpec((n_tensor, chunk, rows), lambda i, where_ref: (0, 0, 0)),
                pl.BlockSpec((rows, tok), fixed),
            ],
            scratch_shapes=[pltpu.VMEM((tok, rows), F32)],
        ),
        out_shape=[
            jax.ShapeDtypeStruct((tok, rows), BF16),
            jax.ShapeDtypeStruct((n_tensor, chunk, rows), BF16),
            jax.ShapeDtypeStruct((rows, tok), BF16),
        ],
        name="project",
    )(where, hidden, qk_scale, cotangent, *[parts[s][r] for r in range(n_blocks) for s in range(2)])


def weight_grad(d_t, hidden, where, n_blocks, odd, dtype):
    rows, tok = d_t.shape
    width = hidden.shape[1] // n_blocks

    def body(where_ref, d_ref, h_ref, out_ref):
        out_ref[0] = jnp.dot(d_ref[...], h_ref[...], preferred_element_type=F32).astype(dtype)

    return pl.pallas_call(
        body,
        grid_spec=pltpu.PrefetchScalarGridSpec(
            num_scalar_prefetch=1,
            grid=(n_blocks // 2,),
            in_specs=[
                pl.BlockSpec((rows, tok), lambda i, where_ref: (0, 0)),
                pl.BlockSpec((tok, width), lambda i, where_ref: (0, where_ref[0] ^ (2 * i + odd))),
            ],
            out_specs=pl.BlockSpec((1, rows, width), lambda i, where_ref: (i, 0, 0)),
        ),
        out_shape=jax.ShapeDtypeStruct((n_blocks // 2, rows, width), dtype),
        name="weight_grad_odd" if odd else "weight_grad_even",
    )(where, d_t, hidden)


def shift(x, by, n_tensor):
    return lax.ppermute(x, "tensor", [(i, (i - by) % n_tensor) for i in range(n_tensor)])


def hidden_share(d_slots, parts, blocks):
    n_tensor, chunk, rows = d_slots.shape
    half, width = parts[0][0].shape

    def body(d_ref, *rest):
        w_refs, out_ref = rest[:-1], rest[-1]
        step = pl.program_id(0)
        d = d_ref[...].reshape(n_tensor * chunk, rows)
        for i in range(len(blocks)):

            @pl.when(step == i)
            def _():
                w = jnp.concatenate([w_refs[2 * i][...], w_refs[2 * i + 1][...]], 0)
                out = jnp.dot(d, w, preferred_element_type=F32).astype(BF16)
                out_ref[...] = out.reshape(n_tensor, chunk, width)

    return pl.pallas_call(
        body,
        grid=(len(blocks),),
        in_specs=[pl.BlockSpec(d_slots.shape, lambda i: (0, 0, 0))]
        + [pl.BlockSpec((half, width), lambda i: (0, 0))] * (2 * len(blocks)),
        out_specs=pl.BlockSpec((n_tensor, chunk, width), lambda i: (0, 0, i)),
        out_shape=jax.ShapeDtypeStruct((n_tensor, chunk, len(blocks) * width), BF16),
        name="hidden_share",
    )(d_slots, *[parts[s][r] for r in blocks for s in range(2)])


def hidden_grad(d_own, d_pair, d_mid, parts, pair, mid, where, blocks, into):
    chunk = d_own.shape[0]
    half, width = parts[0][0].shape
    n_blocks = len(parts[0])
    per = 4

    def body(where_ref, *rest):
        d_refs = rest[:3]
        w_refs = rest[3 : 3 + per * len(blocks)]
        out_ref = rest[-1]
        step = pl.program_id(0)
        for i in range(len(blocks)):

            @pl.when(step == i)
            def _():
                mine = w_refs[per * i : per * (i + 1)]
                w = jnp.concatenate([mine[0][...], mine[1][...]], 0)
                total = jnp.dot(d_refs[0][...], w, preferred_element_type=F32)
                for k in (1, 2):
                    total += jnp.dot(d_refs[k][...], mine[k + 1][...], preferred_element_type=F32)
                out_ref[...] = total.astype(BF16)

    fixed = lambda i, where_ref: (0, 0)

    def column(i, where_ref):
        r = blocks[-1]
        for at in range(len(blocks) - 2, -1, -1):
            r = jnp.where(i == at, blocks[at], r)
        return (0, where_ref[0] ^ r)

    operands = [d_own, d_pair, d_mid]
    for r in blocks:
        operands += [parts[0][r], parts[1][r], pair[r], mid[r]]
    specs = [pl.BlockSpec(x.shape, fixed) for x in operands]
    aliases = {}
    if into is not None:
        operands.append(into)
        specs.append(pl.BlockSpec(memory_space=pl.ANY))
        aliases = {len(operands): 0}
    return pl.pallas_call(
        body,
        grid_spec=pltpu.PrefetchScalarGridSpec(
            num_scalar_prefetch=1,
            grid=(len(blocks),),
            in_specs=specs,
            out_specs=pl.BlockSpec((chunk, width), column),
        ),
        out_shape=jax.ShapeDtypeStruct((chunk, n_blocks * width), BF16),
        input_output_aliases=aliases,
        name="hidden_grad",
    )(where, *operands)


def add_shares(shares, where, blocks, width, into):
    chunk = shares[0].shape[0]

    def body(where_ref, *rest):
        total = rest[0][...].astype(F32)
        for ref in rest[1 : len(shares)]:
            total += ref[...].astype(F32)
        rest[-1][...] = total.astype(BF16)

    def column(i, where_ref):
        r = blocks[-1]
        for at in range(len(blocks) - 2, -1, -1):
            r = jnp.where(i == at, blocks[at], r)
        return (0, where_ref[0] ^ r)

    return pl.pallas_call(
        body,
        grid_spec=pltpu.PrefetchScalarGridSpec(
            num_scalar_prefetch=1,
            grid=(len(blocks),),
            in_specs=[pl.BlockSpec((chunk, width), lambda i, where_ref: (0, i))] * len(shares)
            + [pl.BlockSpec(memory_space=pl.ANY)],
            out_specs=pl.BlockSpec((chunk, width), column),
        ),
        out_shape=jax.ShapeDtypeStruct(into.shape, BF16),
        input_output_aliases={len(shares) + 1: 0},
        name="add_shares",
    )(where, *shares, into)


def halve(part, axis, bit, n_dp):
    go = lax.index_in_dim(part, 1, axis, keepdims=False).astype(BF16)
    stay = lax.index_in_dim(part, 0, axis, keepdims=False)
    return stay, swap(go, bit, n_dp)


def local(hidden, weight, qk_scale, cotangent, n_dp, n_tensor):
    width = weight.shape[1]
    half = weight.shape[0] // 2
    where = jnp.stack([lax.axis_index("dp"), lax.axis_index("tensor")]).astype(jnp.int32)
    ahead = shift(weight, 1, n_tensor)
    behind = shift(weight, -1, n_tensor)
    parts = gather_links(weight, n_dp)
    last = n_dp - 2
    final = [have[last] for have in parts]
    parts = [add_core({r: x for r, x in have.items() if r != last}, n_dp) for have in parts]
    final, ahead, behind = lax.optimization_barrier((final, ahead, behind))
    for have, x in zip(parts, final):
        have.update(add_core({last: x}, n_dp))
    pair = {0: jnp.concatenate([ahead, behind], 0)}
    across = shift(weight, 2, n_tensor)
    bits = [1 << i for i in range(1, n_dp.bit_length() - 1)]
    pair.update({bit: swap(pair[0], bit, n_dp) for bit in bits})
    keys_values, d_slots, d_t = project(hidden, parts, qk_scale, cotangent, where, n_tensor)
    near = [0, 1]
    linked = [r for bit in bits for r in (bit, bit ^ 1)]
    far = [r for r in range(n_dp) if r not in near and r not in linked]
    share = hidden_share(d_slots, parts, far)
    d_rest = [shift(d_slots[k], k, n_tensor) for k in range(1, n_tensor)]
    d_t, share = lax.optimization_barrier((d_t, share))
    cut = share.shape[2] // 2
    via_ahead = shift(share[2, :, :cut], 1, n_tensor)
    via_behind = shift(share[2, :, cut:], -1, n_tensor)
    sent = weight_grad(d_t, hidden, where, n_dp, 1, BF16)
    due = (d_t, sent, pair, via_ahead, via_behind, across)
    d_t, sent, pair, via_ahead, via_behind, across = lax.optimization_barrier(due)
    to_ahead = jnp.concatenate([share[1, :, :cut] + via_ahead, share[1, :, cut:]], 1)
    to_behind = jnp.concatenate([share[-1, :, :cut], share[-1, :, cut:] + via_behind], 1)
    from_ahead, from_behind = shift(to_ahead, 1, n_tensor), shift(to_behind, -1, n_tensor)
    mid = {0: across}
    mid.update({bit: swap(mid[0], bit, n_dp) for bit in bits})
    pair = add_core(pair, n_dp)
    keep = weight_grad(d_t, hidden, where, n_dp, 0, F32)
    total = keep + swap(sent, 1, n_dp).astype(F32)
    total, mid, d_rest = lax.optimization_barrier((total, mid, d_rest))
    mid = add_core(mid, n_dp)
    d_pair = jnp.concatenate([d_rest[0], d_rest[-1]], 1)
    d_all = (d_slots[0], d_pair, d_rest[1], parts, pair, mid, where)
    input_grad = hidden_grad(*d_all, near, None)
    count = len(bits)
    total = total.reshape((2,) * count + total.shape[1:])
    sides = [total[..., :half, :], total[..., half:, :]]
    orders = [list(range(count)), list(range(count))[::-1]]
    left = [list(range(count))[::-1], list(range(count))[::-1]]
    for step in range(count):
        for at in range(2):
            b = orders[at][step]
            axis = left[at].index(b)
            left[at].remove(b)
            sides[at] = halve(sides[at], axis, bits[b], n_dp)
        if step == count - 1:
            input_grad = hidden_grad(*d_all, linked, input_grad)
        if step == count - 2:
            due = (sides, input_grad, from_ahead, from_behind)
            sides, input_grad, from_ahead, from_behind = lax.optimization_barrier(due)
        else:
            sides, input_grad = lax.optimization_barrier((sides, input_grad))
        sides = [stay + came.astype(F32) for stay, came in sides]
    grad = jnp.concatenate(sides, 0)
    input_grad = add_shares([share[0], from_ahead, from_behind], where, far, width, input_grad)
    w = weight.astype(F32)
    sums = jnp.stack([jnp.sum(grad * w, 1), jnp.sum(w * w, 1), jnp.sum(grad * grad, 1)])
    bit = 1
    while bit < n_dp:
        sums = sums + swap(sums, bit, n_dp)
        bit *= 2
    gw, ww, gg = sums[0], sums[1], sums[2]
    ratio = gw / ww
    rate = step_rate * jnp.sqrt(ww / (gg + epsilon))
    norm_sq = ww + rate * rate * (gg - ratio * gw)
    scale = math.sqrt(n_dp * weight.shape[1]) / jnp.sqrt(norm_sq)
    moved = w - rate[:, None] * (grad - ratio[:, None] * w)
    new_weight = (scale[:, None] * moved).astype(BF16)
    return (keys_values, input_grad, new_weight)


def solution(mesh):
    in_specs = (P("dp", None), P("tensor", "dp"), P("tensor", None), P("dp", "tensor"))
    out_specs = (P("dp", "tensor"), P(("dp", "tensor"), None), P("tensor", "dp"))
    n_dp, n_tensor = mesh.shape["dp"], mesh.shape["tensor"]

    def body(hidden, weight, qk_scale, cotangent):
        return local(hidden, weight, qk_scale, cotangent, n_dp, n_tensor)

    return jax.shard_map(body, mesh=mesh, in_specs=in_specs, out_specs=out_specs, check_vma=False)
```

```python
import math

import jax
import jax.numpy as jnp
from jax import lax
from jax.experimental import pallas as pl
from jax.experimental.pallas import tpu as pltpu
from jax.sharding import PartitionSpec as P

step_rate = 0.5
epsilon = 1e-06
F32 = jnp.float32
BF16 = jnp.bfloat16


def swap(x, bit, n_dp):
    return lax.ppermute(x, "dp", [(i, i ^ bit) for i in range(n_dp)])


def gather_links(w, n_dp):
    bits = [1 << i for i in range(1, n_dp.bit_length() - 1)]
    half = w.shape[0] // 2
    parts = []
    for rows, order in ((w[:half], bits), (w[half:], bits[::-1])):
        have = {0: rows}
        for bit in order:
            have.update({r ^ bit: swap(x, bit, n_dp) for r, x in list(have.items())})
        parts.append(have)
    return parts


def add_core(have, n_dp):
    return {**have, **{r ^ 1: swap(x, 1, n_dp) for r, x in have.items()}}


def project(hidden, parts, qk_scale, cotangent, where, n_tensor):
    tok = hidden.shape[0]
    n_blocks = len(parts[0])
    half, width = parts[0][0].shape
    rows = 2 * half
    heads, size = qk_scale.shape
    chunk = tok // n_tensor

    def body(where_ref, h_ref, s_ref, c_ref, *rest):
        w_refs = rest[: 2 * n_blocks]
        out_ref, d_ref, dt_ref, acc = rest[2 * n_blocks :]
        step = pl.program_id(0)
        for r in range(n_blocks):

            @pl.when(step == r)
            def _():
                w = jnp.concatenate([w_refs[2 * r][...], w_refs[2 * r + 1][...]], 0)
                part = lax.dot_general(h_ref[...], w, (((1,), (1,)), ((), ())), preferred_element_type=F32)
                if r == 0:
                    acc[...] = part
                else:
                    acc[...] += part

        @pl.when(step == n_blocks - 1)
        def _():
            for h in range(heads):
                k_at = slice(2 * h * size, (2 * h + 1) * size)
                v_at = slice((2 * h + 1) * size, (2 * h + 2) * size)
                key_raw = acc[:, k_at]
                length = jnp.sqrt(jnp.sum(key_raw * key_raw, -1, keepdims=True) + epsilon)
                unit = key_raw / length
                factor = s_ref[h : h + 1, :] * math.sqrt(size)
                out_ref[:, k_at] = (factor * unit).astype(BF16)
                out_ref[:, v_at] = acc[:, v_at].astype(BF16)
                along = factor * c_ref[:, k_at].astype(F32)
                grad = (along - unit * jnp.sum(unit * along, -1, keepdims=True)) / length
                for j in range(n_tensor):
                    slot = lax.rem(where_ref[1] + (n_tensor - j), n_tensor)
                    at = slice(j * chunk, (j + 1) * chunk)
                    d_ref[slot, :, k_at] = grad[at].astype(BF16)
                    d_ref[slot, :, v_at] = c_ref[at, v_at]
                dt_ref[k_at, :] = grad.T.astype(BF16)
                dt_ref[v_at, :] = c_ref[:, v_at].astype(F32).T.astype(BF16)

    fixed = lambda i, where_ref: (0, 0)
    return pl.pallas_call(
        body,
        grid_spec=pltpu.PrefetchScalarGridSpec(
            num_scalar_prefetch=1,
            grid=(n_blocks,),
            in_specs=[
                pl.BlockSpec((tok, width), lambda i, where_ref: (0, where_ref[0] ^ i)),
                pl.BlockSpec((heads, size), fixed),
                pl.BlockSpec((tok, rows), fixed),
            ]
            + [pl.BlockSpec((half, width), fixed)] * (2 * n_blocks),
            out_specs=[
                pl.BlockSpec((tok, rows), fixed),
                pl.BlockSpec((n_tensor, chunk, rows), lambda i, where_ref: (0, 0, 0)),
                pl.BlockSpec((rows, tok), fixed),
            ],
            scratch_shapes=[pltpu.VMEM((tok, rows), F32)],
        ),
        out_shape=[
            jax.ShapeDtypeStruct((tok, rows), BF16),
            jax.ShapeDtypeStruct((n_tensor, chunk, rows), BF16),
            jax.ShapeDtypeStruct((rows, tok), BF16),
        ],
        name="project",
    )(where, hidden, qk_scale, cotangent, *[parts[s][r] for r in range(n_blocks) for s in range(2)])


def weight_grad(d_t, hidden, where, n_blocks, odd, dtype):
    rows, tok = d_t.shape
    width = hidden.shape[1] // n_blocks

    def body(where_ref, d_ref, h_ref, out_ref):
        out_ref[0] = jnp.dot(d_ref[...], h_ref[...], preferred_element_type=F32).astype(dtype)

    return pl.pallas_call(
        body,
        grid_spec=pltpu.PrefetchScalarGridSpec(
            num_scalar_prefetch=1,
            grid=(n_blocks // 2,),
            in_specs=[
                pl.BlockSpec((rows, tok), lambda i, where_ref: (0, 0)),
                pl.BlockSpec((tok, width), lambda i, where_ref: (0, where_ref[0] ^ (2 * i + odd))),
            ],
            out_specs=pl.BlockSpec((1, rows, width), lambda i, where_ref: (i, 0, 0)),
        ),
        out_shape=jax.ShapeDtypeStruct((n_blocks // 2, rows, width), dtype),
        name="weight_grad_odd" if odd else "weight_grad_even",
    )(where, d_t, hidden)


def shift(x, by, n_tensor):
    return lax.ppermute(x, "tensor", [(i, (i - by) % n_tensor) for i in range(n_tensor)])


def hidden_share(d_slots, parts, blocks):
    n_tensor, chunk, rows = d_slots.shape
    half, width = parts[0][0].shape

    def body(d_ref, *rest):
        w_refs, out_ref = rest[:-1], rest[-1]
        step = pl.program_id(0)
        d = d_ref[...].reshape(n_tensor * chunk, rows)
        for i in range(len(blocks)):

            @pl.when(step == i)
            def _():
                w = jnp.concatenate([w_refs[2 * i][...], w_refs[2 * i + 1][...]], 0)
                out = jnp.dot(d, w, preferred_element_type=F32).astype(BF16)
                out_ref[...] = out.reshape(n_tensor, chunk, width)

    return pl.pallas_call(
        body,
        grid=(len(blocks),),
        in_specs=[pl.BlockSpec(d_slots.shape, lambda i: (0, 0, 0))]
        + [pl.BlockSpec((half, width), lambda i: (0, 0))] * (2 * len(blocks)),
        out_specs=pl.BlockSpec((n_tensor, chunk, width), lambda i: (0, 0, i)),
        out_shape=jax.ShapeDtypeStruct((n_tensor, chunk, len(blocks) * width), BF16),
        name="hidden_share",
    )(d_slots, *[parts[s][r] for r in blocks for s in range(2)])


def hidden_grad(d_own, d_pair, d_mid, parts, pair, mid, where, blocks, into):
    chunk = d_own.shape[0]
    half, width = parts[0][0].shape
    n_blocks = len(parts[0])
    per = 4

    def body(where_ref, *rest):
        d_refs = rest[:3]
        w_refs = rest[3 : 3 + per * len(blocks)]
        out_ref = rest[-1]
        step = pl.program_id(0)
        for i in range(len(blocks)):

            @pl.when(step == i)
            def _():
                mine = w_refs[per * i : per * (i + 1)]
                w = jnp.concatenate([mine[0][...], mine[1][...]], 0)
                total = jnp.dot(d_refs[0][...], w, preferred_element_type=F32)
                for k in (1, 2):
                    total += jnp.dot(d_refs[k][...], mine[k + 1][...], preferred_element_type=F32)
                out_ref[...] = total.astype(BF16)

    fixed = lambda i, where_ref: (0, 0)

    def column(i, where_ref):
        r = blocks[-1]
        for at in range(len(blocks) - 2, -1, -1):
            r = jnp.where(i == at, blocks[at], r)
        return (0, where_ref[0] ^ r)

    operands = [d_own, d_pair, d_mid]
    for r in blocks:
        operands += [parts[0][r], parts[1][r], pair[r], mid[r]]
    specs = [pl.BlockSpec(x.shape, fixed) for x in operands]
    aliases = {}
    if into is not None:
        operands.append(into)
        specs.append(pl.BlockSpec(memory_space=pl.ANY))
        aliases = {len(operands): 0}
    return pl.pallas_call(
        body,
        grid_spec=pltpu.PrefetchScalarGridSpec(
            num_scalar_prefetch=1,
            grid=(len(blocks),),
            in_specs=specs,
            out_specs=pl.BlockSpec((chunk, width), column),
        ),
        out_shape=jax.ShapeDtypeStruct((chunk, n_blocks * width), BF16),
        input_output_aliases=aliases,
        name="hidden_grad",
    )(where, *operands)


def add_shares(shares, where, blocks, width, into):
    chunk = shares[0].shape[0]

    def body(where_ref, *rest):
        total = rest[0][...].astype(F32)
        for ref in rest[1 : len(shares)]:
            total += ref[...].astype(F32)
        rest[-1][...] = total.astype(BF16)

    def column(i, where_ref):
        r = blocks[-1]
        for at in range(len(blocks) - 2, -1, -1):
            r = jnp.where(i == at, blocks[at], r)
        return (0, where_ref[0] ^ r)

    return pl.pallas_call(
        body,
        grid_spec=pltpu.PrefetchScalarGridSpec(
            num_scalar_prefetch=1,
            grid=(len(blocks),),
            in_specs=[pl.BlockSpec((chunk, width), lambda i, where_ref: (0, i))] * len(shares)
            + [pl.BlockSpec(memory_space=pl.ANY)],
            out_specs=pl.BlockSpec((chunk, width), column),
        ),
        out_shape=jax.ShapeDtypeStruct(into.shape, BF16),
        input_output_aliases={len(shares) + 1: 0},
        name="add_shares",
    )(where, *shares, into)


def halve(part, axis, bit, n_dp):
    go = lax.index_in_dim(part, 1, axis, keepdims=False).astype(BF16)
    stay = lax.index_in_dim(part, 0, axis, keepdims=False)
    return stay, swap(go, bit, n_dp)


def local(hidden, weight, qk_scale, cotangent, n_dp, n_tensor):
    width = weight.shape[1]
    half = weight.shape[0] // 2
    where = jnp.stack([lax.axis_index("dp"), lax.axis_index("tensor")]).astype(jnp.int32)
    ahead = shift(weight, 1, n_tensor)
    behind = shift(weight, -1, n_tensor)
    parts = gather_links(weight, n_dp)
    last = n_dp - 2
    final = [have[last] for have in parts]
    parts = [add_core({r: x for r, x in have.items() if r != last}, n_dp) for have in parts]
    final, ahead, behind = lax.optimization_barrier((final, ahead, behind))
    for have, x in zip(parts, final):
        have.update(add_core({last: x}, n_dp))
    pair = {0: jnp.concatenate([ahead, behind], 0)}
    across = shift(weight, 2, n_tensor)
    bits = [1 << i for i in range(1, n_dp.bit_length() - 1)]
    pair.update({bit: swap(pair[0], bit, n_dp) for bit in bits})
    keys_values, d_slots, d_t = project(hidden, parts, qk_scale, cotangent, where, n_tensor)
    near = [0, 1]
    linked = [r for bit in bits for r in (bit, bit ^ 1)]
    far = [r for r in range(n_dp) if r not in near and r not in linked]
    share = hidden_share(d_slots, parts, far)
    d_rest = [shift(d_slots[k], k, n_tensor) for k in range(1, n_tensor)]
    d_t, share = lax.optimization_barrier((d_t, share))
    cut = share.shape[2] // 2
    via_ahead = shift(share[2, :, :cut], 1, n_tensor)
    via_behind = shift(share[2, :, cut:], -1, n_tensor)
    sent = weight_grad(d_t, hidden, where, n_dp, 1, BF16)
    due = (d_t, sent, pair, via_ahead, via_behind, across)
    d_t, sent, pair, via_ahead, via_behind, across = lax.optimization_barrier(due)
    to_ahead = jnp.concatenate([share[1, :, :cut] + via_ahead, share[1, :, cut:]], 1)
    to_behind = jnp.concatenate([share[-1, :, :cut], share[-1, :, cut:] + via_behind], 1)
    from_ahead, from_behind = shift(to_ahead, 1, n_tensor), shift(to_behind, -1, n_tensor)
    mid = {0: across}
    mid.update({bit: swap(mid[0], bit, n_dp) for bit in bits})
    pair = add_core(pair, n_dp)
    keep = weight_grad(d_t, hidden, where, n_dp, 0, F32)
    total = keep + swap(sent, 1, n_dp).astype(F32)
    total, mid, d_rest = lax.optimization_barrier((total, mid, d_rest))
    mid = add_core(mid, n_dp)
    d_pair = jnp.concatenate([d_rest[0], d_rest[-1]], 1)
    d_all = (d_slots[0], d_pair, d_rest[1], parts, pair, mid, where)
    input_grad = hidden_grad(*d_all, near, None)
    count = len(bits)
    total = total.reshape((2,) * count + total.shape[1:])
    sides = [total[..., :half, :], total[..., half:, :]]
    orders = [list(range(count)), list(range(count))[::-1]]
    left = [list(range(count))[::-1], list(range(count))[::-1]]
    for step in range(count):
        for at in range(2):
            b = orders[at][step]
            axis = left[at].index(b)
            left[at].remove(b)
            sides[at] = halve(sides[at], axis, bits[b], n_dp)
        if step == count - 1:
            input_grad = hidden_grad(*d_all, linked, input_grad)
        kept = [stay for stay, came in sides]
        came = [came for stay, came in sides]
        if step == count - 2:
            came, input_grad, from_ahead = lax.optimization_barrier((came, input_grad, from_ahead))
        elif step == count - 1:
            came, input_grad, from_behind = lax.optimization_barrier((came, input_grad, from_behind))
        sides = [stay + x.astype(F32) for stay, x in zip(kept, came)]
    grad = jnp.concatenate(sides, 0)
    input_grad = add_shares([share[0], from_ahead, from_behind], where, far, width, input_grad)
    w = weight.astype(F32)
    sums = jnp.stack([jnp.sum(grad * w, 1), jnp.sum(w * w, 1), jnp.sum(grad * grad, 1)])
    bit = 1
    while bit < n_dp:
        sums = sums + swap(sums, bit, n_dp)
        bit *= 2
    gw, ww, gg = sums[0], sums[1], sums[2]
    ratio = gw / ww
    rate = step_rate * jnp.sqrt(ww / (gg + epsilon))
    norm_sq = ww + rate * rate * (gg - ratio * gw)
    scale = math.sqrt(n_dp * weight.shape[1]) / jnp.sqrt(norm_sq)
    moved = w - rate[:, None] * (grad - ratio[:, None] * w)
    new_weight = (scale[:, None] * moved).astype(BF16)
    return (keys_values, input_grad, new_weight)


def solution(mesh):
    in_specs = (P("dp", None), P("tensor", "dp"), P("tensor", None), P("dp", "tensor"))
    out_specs = (P("dp", "tensor"), P(("dp", "tensor"), None), P("tensor", "dp"))
    n_dp, n_tensor = mesh.shape["dp"], mesh.shape["tensor"]

    def body(hidden, weight, qk_scale, cotangent):
        return local(hidden, weight, qk_scale, cotangent, n_dp, n_tensor)

    return jax.shard_map(body, mesh=mesh, in_specs=in_specs, out_specs=out_specs, check_vma=False)
```

```python
import math

import jax
import jax.numpy as jnp
from jax import lax
from jax.experimental import pallas as pl
from jax.experimental.pallas import tpu as pltpu
from jax.sharding import PartitionSpec as P

step_rate = 0.5
epsilon = 1e-06
F32 = jnp.float32
BF16 = jnp.bfloat16


def swap(x, bit, n_dp):
    return lax.ppermute(x, "dp", [(i, i ^ bit) for i in range(n_dp)])


def gather_links(w, n_dp):
    bits = [1 << i for i in range(1, n_dp.bit_length() - 1)]
    half = w.shape[0] // 2
    parts = []
    for rows, order in ((w[:half], bits), (w[half:], bits[::-1])):
        have = {0: rows}
        for bit in order:
            have.update({r ^ bit: swap(x, bit, n_dp) for r, x in list(have.items())})
        parts.append(have)
    return parts


def add_core(have, n_dp):
    return {**have, **{r ^ 1: swap(x, 1, n_dp) for r, x in have.items()}}


def project(hidden, parts, qk_scale, cotangent, where, n_tensor):
    tok = hidden.shape[0]
    n_blocks = len(parts[0])
    half, width = parts[0][0].shape
    rows = 2 * half
    heads, size = qk_scale.shape
    chunk = tok // n_tensor

    def body(where_ref, h_ref, s_ref, c_ref, *rest):
        w_refs = rest[: 2 * n_blocks]
        out_ref, d_ref, dt_ref, acc = rest[2 * n_blocks :]
        step = pl.program_id(0)
        for r in range(n_blocks):

            @pl.when(step == r)
            def _():
                w = jnp.concatenate([w_refs[2 * r][...], w_refs[2 * r + 1][...]], 0)
                part = lax.dot_general(h_ref[...], w, (((1,), (1,)), ((), ())), preferred_element_type=F32)
                if r == 0:
                    acc[...] = part
                else:
                    acc[...] += part

        @pl.when(step == n_blocks - 1)
        def _():
            for h in range(heads):
                k_at = slice(2 * h * size, (2 * h + 1) * size)
                v_at = slice((2 * h + 1) * size, (2 * h + 2) * size)
                key_raw = acc[:, k_at]
                length = jnp.sqrt(jnp.sum(key_raw * key_raw, -1, keepdims=True) + epsilon)
                unit = key_raw / length
                factor = s_ref[h : h + 1, :] * math.sqrt(size)
                out_ref[:, k_at] = (factor * unit).astype(BF16)
                out_ref[:, v_at] = acc[:, v_at].astype(BF16)
                along = factor * c_ref[:, k_at].astype(F32)
                grad = (along - unit * jnp.sum(unit * along, -1, keepdims=True)) / length
                for j in range(n_tensor):
                    slot = lax.rem(where_ref[1] + (n_tensor - j), n_tensor)
                    at = slice(j * chunk, (j + 1) * chunk)
                    d_ref[slot, :, k_at] = grad[at].astype(BF16)
                    d_ref[slot, :, v_at] = c_ref[at, v_at]
                dt_ref[k_at, :] = grad.T.astype(BF16)
                dt_ref[v_at, :] = c_ref[:, v_at].astype(F32).T.astype(BF16)

    fixed = lambda i, where_ref: (0, 0)
    return pl.pallas_call(
        body,
        grid_spec=pltpu.PrefetchScalarGridSpec(
            num_scalar_prefetch=1,
            grid=(n_blocks,),
            in_specs=[
                pl.BlockSpec((tok, width), lambda i, where_ref: (0, where_ref[0] ^ i)),
                pl.BlockSpec((heads, size), fixed),
                pl.BlockSpec((tok, rows), fixed),
            ]
            + [pl.BlockSpec((half, width), fixed)] * (2 * n_blocks),
            out_specs=[
                pl.BlockSpec((tok, rows), fixed),
                pl.BlockSpec((n_tensor, chunk, rows), lambda i, where_ref: (0, 0, 0)),
                pl.BlockSpec((rows, tok), fixed),
            ],
            scratch_shapes=[pltpu.VMEM((tok, rows), F32)],
        ),
        out_shape=[
            jax.ShapeDtypeStruct((tok, rows), BF16),
            jax.ShapeDtypeStruct((n_tensor, chunk, rows), BF16),
            jax.ShapeDtypeStruct((rows, tok), BF16),
        ],
        name="project",
    )(where, hidden, qk_scale, cotangent, *[parts[s][r] for r in range(n_blocks) for s in range(2)])


def weight_grad(d_t, hidden, where, n_blocks, odd, dtype):
    rows, tok = d_t.shape
    width = hidden.shape[1] // n_blocks

    def body(where_ref, d_ref, h_ref, out_ref):
        out_ref[0] = jnp.dot(d_ref[...], h_ref[...], preferred_element_type=F32).astype(dtype)

    return pl.pallas_call(
        body,
        grid_spec=pltpu.PrefetchScalarGridSpec(
            num_scalar_prefetch=1,
            grid=(n_blocks // 2,),
            in_specs=[
                pl.BlockSpec((rows, tok), lambda i, where_ref: (0, 0)),
                pl.BlockSpec((tok, width), lambda i, where_ref: (0, where_ref[0] ^ (2 * i + odd))),
            ],
            out_specs=pl.BlockSpec((1, rows, width), lambda i, where_ref: (i, 0, 0)),
        ),
        out_shape=jax.ShapeDtypeStruct((n_blocks // 2, rows, width), dtype),
        name="weight_grad_odd" if odd else "weight_grad_even",
    )(where, d_t, hidden)


def shift(x, by, n_tensor):
    return lax.ppermute(x, "tensor", [(i, (i - by) % n_tensor) for i in range(n_tensor)])


def hidden_share(d_slots, parts, blocks):
    n_tensor, chunk, rows = d_slots.shape
    half, width = parts[0][0].shape

    def body(d_ref, *rest):
        w_refs, out_ref = rest[:-1], rest[-1]
        step = pl.program_id(0)
        d = d_ref[...].reshape(n_tensor * chunk, rows)
        for i in range(len(blocks)):

            @pl.when(step == i)
            def _():
                w = jnp.concatenate([w_refs[2 * i][...], w_refs[2 * i + 1][...]], 0)
                out = jnp.dot(d, w, preferred_element_type=F32).astype(BF16)
                out_ref[...] = out.reshape(n_tensor, chunk, width)

    return pl.pallas_call(
        body,
        grid=(len(blocks),),
        in_specs=[pl.BlockSpec(d_slots.shape, lambda i: (0, 0, 0))]
        + [pl.BlockSpec((half, width), lambda i: (0, 0))] * (2 * len(blocks)),
        out_specs=pl.BlockSpec((n_tensor, chunk, width), lambda i: (0, 0, i)),
        out_shape=jax.ShapeDtypeStruct((n_tensor, chunk, len(blocks) * width), BF16),
        name="hidden_share",
    )(d_slots, *[parts[s][r] for r in blocks for s in range(2)])


def hidden_grad(d_own, d_pair, d_mid, parts, pair, mid, where, blocks, into):
    chunk = d_own.shape[0]
    half, width = parts[0][0].shape
    n_blocks = len(parts[0])
    per = 4

    def body(where_ref, *rest):
        d_refs = rest[:3]
        w_refs = rest[3 : 3 + per * len(blocks)]
        out_ref = rest[-1]
        step = pl.program_id(0)
        for i in range(len(blocks)):

            @pl.when(step == i)
            def _():
                mine = w_refs[per * i : per * (i + 1)]
                w = jnp.concatenate([mine[0][...], mine[1][...]], 0)
                total = jnp.dot(d_refs[0][...], w, preferred_element_type=F32)
                for k in (1, 2):
                    total += jnp.dot(d_refs[k][...], mine[k + 1][...], preferred_element_type=F32)
                out_ref[...] = total.astype(BF16)

    fixed = lambda i, where_ref: (0, 0)

    def column(i, where_ref):
        r = blocks[-1]
        for at in range(len(blocks) - 2, -1, -1):
            r = jnp.where(i == at, blocks[at], r)
        return (0, where_ref[0] ^ r)

    operands = [d_own, d_pair, d_mid]
    for r in blocks:
        operands += [parts[0][r], parts[1][r], pair[r], mid[r]]
    specs = [pl.BlockSpec(x.shape, fixed) for x in operands]
    aliases = {}
    if into is not None:
        operands.append(into)
        specs.append(pl.BlockSpec(memory_space=pl.ANY))
        aliases = {len(operands): 0}
    return pl.pallas_call(
        body,
        grid_spec=pltpu.PrefetchScalarGridSpec(
            num_scalar_prefetch=1,
            grid=(len(blocks),),
            in_specs=specs,
            out_specs=pl.BlockSpec((chunk, width), column),
        ),
        out_shape=jax.ShapeDtypeStruct((chunk, n_blocks * width), BF16),
        input_output_aliases=aliases,
        name="hidden_grad",
    )(where, *operands)


def add_shares(shares, where, blocks, width, into):
    chunk = shares[0].shape[0]

    def body(where_ref, *rest):
        total = rest[0][...].astype(F32)
        for ref in rest[1 : len(shares)]:
            total += ref[...].astype(F32)
        rest[-1][...] = total.astype(BF16)

    def column(i, where_ref):
        r = blocks[-1]
        for at in range(len(blocks) - 2, -1, -1):
            r = jnp.where(i == at, blocks[at], r)
        return (0, where_ref[0] ^ r)

    return pl.pallas_call(
        body,
        grid_spec=pltpu.PrefetchScalarGridSpec(
            num_scalar_prefetch=1,
            grid=(len(blocks),),
            in_specs=[pl.BlockSpec((chunk, width), lambda i, where_ref: (0, i))] * len(shares)
            + [pl.BlockSpec(memory_space=pl.ANY)],
            out_specs=pl.BlockSpec((chunk, width), column),
        ),
        out_shape=jax.ShapeDtypeStruct(into.shape, BF16),
        input_output_aliases={len(shares) + 1: 0},
        name="add_shares",
    )(where, *shares, into)


def halve(part, axis, bit, n_dp):
    go = lax.index_in_dim(part, 1, axis, keepdims=False).astype(BF16)
    stay = lax.index_in_dim(part, 0, axis, keepdims=False)
    return stay, swap(go, bit, n_dp)


def local(hidden, weight, qk_scale, cotangent, n_dp, n_tensor):
    width = weight.shape[1]
    half = weight.shape[0] // 2
    where = jnp.stack([lax.axis_index("dp"), lax.axis_index("tensor")]).astype(jnp.int32)
    ahead = shift(weight, 1, n_tensor)
    behind = shift(weight, -1, n_tensor)
    parts = gather_links(weight, n_dp)
    last = n_dp - 2
    final = [have[last] for have in parts]
    parts = [add_core({r: x for r, x in have.items() if r != last}, n_dp) for have in parts]
    final, ahead, behind = lax.optimization_barrier((final, ahead, behind))
    for have, x in zip(parts, final):
        have.update(add_core({last: x}, n_dp))
    pair = {0: jnp.concatenate([ahead, behind], 0)}
    across = shift(weight, 2, n_tensor)
    bits = [1 << i for i in range(1, n_dp.bit_length() - 1)]
    pair.update({bit: swap(pair[0], bit, n_dp) for bit in bits})
    keys_values, d_slots, d_t = project(hidden, parts, qk_scale, cotangent, where, n_tensor)
    near = [0, 1]
    linked = [r for bit in bits for r in (bit, bit ^ 1)]
    far = [r for r in range(n_dp) if r not in near and r not in linked]
    share = hidden_share(d_slots, parts, far)
    d_rest = [shift(d_slots[k], k, n_tensor) for k in range(1, n_tensor)]
    d_t, share = lax.optimization_barrier((d_t, share))
    cut = share.shape[2] // 2
    via_ahead = shift(share[2, :, :cut], 1, n_tensor)
    via_behind = shift(share[2, :, cut:], -1, n_tensor)
    sent = weight_grad(d_t, hidden, where, n_dp, 1, BF16)
    d_t, sent, pair, across = lax.optimization_barrier((d_t, sent, pair, across))
    mid = {0: across}
    mid.update({bit: swap(mid[0], bit, n_dp) for bit in bits})
    pair = add_core(pair, n_dp)
    keep = weight_grad(d_t, hidden, where, n_dp, 0, F32)
    keep, via_ahead, via_behind = lax.optimization_barrier((keep, via_ahead, via_behind))
    to_ahead = jnp.concatenate([share[1, :, :cut] + via_ahead, share[1, :, cut:]], 1)
    to_behind = jnp.concatenate([share[-1, :, :cut], share[-1, :, cut:] + via_behind], 1)
    from_ahead, from_behind = shift(to_ahead, 1, n_tensor), shift(to_behind, -1, n_tensor)
    total = keep + swap(sent, 1, n_dp).astype(F32)
    total, mid, d_rest = lax.optimization_barrier((total, mid, d_rest))
    mid = add_core(mid, n_dp)
    d_pair = jnp.concatenate([d_rest[0], d_rest[-1]], 1)
    d_all = (d_slots[0], d_pair, d_rest[1], parts, pair, mid, where)
    input_grad = hidden_grad(*d_all, near, None)
    count = len(bits)
    total = total.reshape((2,) * count + total.shape[1:])
    sides = [total[..., :half, :], total[..., half:, :]]
    orders = [list(range(count)), list(range(count))[::-1]]
    left = [list(range(count))[::-1], list(range(count))[::-1]]
    for step in range(count):
        for at in range(2):
            b = orders[at][step]
            axis = left[at].index(b)
            left[at].remove(b)
            sides[at] = halve(sides[at], axis, bits[b], n_dp)
        if step == count - 1:
            input_grad = hidden_grad(*d_all, linked, input_grad)
        kept = [stay for stay, came in sides]
        came = [came for stay, came in sides]
        if step == count - 2:
            came, input_grad, from_ahead = lax.optimization_barrier((came, input_grad, from_ahead))
        elif step == count - 1:
            came, input_grad, from_behind = lax.optimization_barrier((came, input_grad, from_behind))
        sides = [stay + x.astype(F32) for stay, x in zip(kept, came)]
    grad = jnp.concatenate(sides, 0)
    input_grad = add_shares([share[0], from_ahead, from_behind], where, far, width, input_grad)
    w = weight.astype(F32)
    sums = jnp.stack([jnp.sum(grad * w, 1), jnp.sum(w * w, 1), jnp.sum(grad * grad, 1)])
    bit = 1
    while bit < n_dp:
        sums = sums + swap(sums, bit, n_dp)
        bit *= 2
    gw, ww, gg = sums[0], sums[1], sums[2]
    ratio = gw / ww
    rate = step_rate * jnp.sqrt(ww / (gg + epsilon))
    norm_sq = ww + rate * rate * (gg - ratio * gw)
    scale = math.sqrt(n_dp * weight.shape[1]) / jnp.sqrt(norm_sq)
    moved = w - rate[:, None] * (grad - ratio[:, None] * w)
    new_weight = (scale[:, None] * moved).astype(BF16)
    return (keys_values, input_grad, new_weight)


def solution(mesh):
    in_specs = (P("dp", None), P("tensor", "dp"), P("tensor", None), P("dp", "tensor"))
    out_specs = (P("dp", "tensor"), P(("dp", "tensor"), None), P("tensor", "dp"))
    n_dp, n_tensor = mesh.shape["dp"], mesh.shape["tensor"]

    def body(hidden, weight, qk_scale, cotangent):
        return local(hidden, weight, qk_scale, cotangent, n_dp, n_tensor)

    return jax.shard_map(body, mesh=mesh, in_specs=in_specs, out_specs=out_specs, check_vma=False)
```
